512 devices in a mesh: lev: 32 (over x_lo, z), mem: 16 (over x_hi, y, core).
Axes of the slice: x: 4 (x_hi: 2, x_lo: 2; x = x_hi * 2 + x_lo), y: 4, z: 16, core: 2. Of those that a mesh axis runs over, the one named last changes fastest.
Arguments:
- control: bfloat16 [32, 5, 128, 4096], P('mem', None, 'lev'), may hold values from -6 to 6
- static_control_vector: bfloat16 [5, 128, 4096], P(None, None, 'lev'), may hold values from -6 to 6
- perturb: bfloat16 [32, 5, 128, 4096], P('mem', None, None, 'lev'), may hold values from -6 to 6
- tiles: bfloat16 [4, 64, 64], replicated, may hold values from -0.375 to 0.375
- block_offset: int32 [64, 4], replicated, may hold values from -8 to 8
- vert: bfloat16 [5, 128, 128], replicated, may hold values from -0.5 to 0.5
- static_vertical_root: bfloat16 [5, 128, 128], replicated, may hold values from -0.5 to 0.5
- obs_index: int32 [524288], P(('lev', 'mem')), may hold values from 0 to 5119
- obs_value: float32 [524288], P(('lev', 'mem')), may hold values from -6 to 6
- obs_sigma: float32 [524288], P(('lev', 'mem')), may hold values from 0.3 to 1
- huber_mask: int32 [524288], P(('lev', 'mem')), may hold values 0 or 1
Outputs:
- control_out: bfloat16 [32, 5, 128, 4096], P('mem', None, 'lev')
- static_out: bfloat16 [5, 128, 4096], P(None, None, 'lev')
The draws below stay inside these ranges and needn't reach their ends.
Inputs may be any that keep to these rules, and one draw needn't show every extreme that they name: `obs_index`: indices count in the block held by the observation's own device: 5 variables, 128 / 16 levels, 128 columns, in that order. `block_offset`: source blocks wrap around the window.
All inputs are finite; a program needn't handle non-finite values. No bound on the sum of `huber_mask` on one device may be relied on, other than what follows from the above.
Results may differ from the reference program's by a relative error of at most 0.0057.
Values may be sent and summed in bfloat16 or wider, within the bound.
No kernel may reach another device: no remote copies, remote signals or barrier semaphores. Data moves between devices by JAX's collectives and lax.ppermute only.
A program may use at most 64 MiB of HBM per device.

```python
import math
import jax
import jax.numpy as jnp
from jax import lax

V = 5
LEVELS = 128
BLOCK = 64
KNB = 4
COL_DEV = 128
ITERS = 2
M = 32
COLS = 4096
NBLK = 64
OBS = 524288
N_LEV = 32
N_MEM = 16


def place_ends(values, key, low, top_value):
    dims = values.shape
    place = [jax.random.randint(jax.random.fold_in(key, axis), (), 0, dims[axis]) for axis in range(len(dims))]
    values = values.at[tuple(place)].set(low)
    longest = dims.index(max(dims))
    place[longest] = (place[longest] + 1) % dims[longest]
    return values.at[tuple(place)].set(top_value)


def shard_levels(stream_key, dims, split, smallest, top_value):
    level = 1.0
    for dim, shards_of in split:
        heights = jax.random.uniform(jax.random.fold_in(jax.random.fold_in(stream_key, 6), dim), (shards_of,), jnp.float32, smallest / len(split), top_value / len(split))
        level = level * jnp.repeat(jnp.exp(heights), dims[dim] // shards_of).reshape((-1,) + (1,) * (len(dims) - 1 - dim))
    return level


def noise(stream_key, shape, spread, limit, pieces=(), kind=jnp.bfloat16):
    entries = spread * jax.random.normal(stream_key, shape, jnp.float32)
    if pieces:
        entries = entries * shard_levels(stream_key, shape, pieces, -0.22, 0.18)
    return jnp.clip(entries, -limit, limit).astype(kind)


def setup_inputs(seed: int = 0) -> dict:
    key_list = jax.random.split(jax.random.key(seed), 12)
    control = noise(key_list[0], (M, V, LEVELS, COLS), 1.0, 6.0, ((0, 16), (2, 32)))
    static_control_vector = noise(key_list[1], (V, LEVELS, COLS), 1.0, 6.0, ((2, 32),))
    perturb = noise(key_list[2], (M, V, LEVELS, COLS), 1.0, 6.0, ((0, 16), (3, 32)))
    tiles = noise(key_list[3], (KNB, BLOCK, BLOCK), (BLOCK * KNB) ** -0.5, 0.375)
    block_offset = place_ends(jax.random.randint(key_list[4], (NBLK, KNB), -8, 9), jax.random.fold_in(key_list[4], 1), -8, 8).astype(jnp.int32)
    vert = noise(key_list[5], (V, LEVELS, LEVELS), LEVELS ** -0.5, 0.5)
    static_vertical_root = noise(key_list[6], (V, LEVELS, LEVELS), LEVELS ** -0.5, 0.5)
    obs_index = place_ends(jax.random.randint(key_list[7], (OBS,), 0, V * (LEVELS // N_MEM) * COL_DEV), jax.random.fold_in(key_list[7], 1), 0, (V * (LEVELS // N_MEM) * COL_DEV) - 1).astype(jnp.int32)
    obs_value = noise(key_list[8], (OBS,), 1.0, 6.0, ((0, 512),), jnp.float32)
    obs_sigma = jnp.clip(jnp.exp(math.log(1.0) - 1.2039728 * jax.random.uniform(key_list[9], (OBS,), jnp.float32) ** shard_levels(key_list[9], (OBS,), ((0, 512),), -0.2, 0.2)), 0.3, 1.0)
    huber_mask = place_ends((jax.random.randint(key_list[10], (OBS,), 0, 4) < 3).astype(jnp.int32), jax.random.fold_in(key_list[10], 1), 0, 1)
    return {"control": control, "static_control_vector": static_control_vector, "perturb": perturb, "tiles": tiles, "block_offset": block_offset, "vert": vert, "static_vertical_root": static_vertical_root, "obs_index": obs_index, "obs_value": obs_value, "obs_sigma": obs_sigma, "huber_mask": huber_mask}


ENS_W = 0.85
STATIC_WEIGHT = 0.5
TAU = 0.5
HUBER_LOW = 0.3

def selectors(block_offset):
    count = block_offset.shape[0]
    blocks = jnp.arange(count, dtype=jnp.int32)
    source = (blocks[:, None] + block_offset) % count
    return (source.T[:, :, None] == blocks[None, None, :]).astype(jnp.float32)

def horizontal(field, tiles, picks):
    shaped = field.astype(jnp.float32).reshape(field.shape[:-1] + (NBLK, BLOCK))
    total = jnp.zeros(shaped.shape, jnp.float32)
    for slot in range(KNB):
        moved = jnp.einsum('bj,...jc->...bc', picks[slot], shaped, precision=lax.Precision.HIGHEST)
        total = total + jnp.einsum('...bc,cd->...bd', moved, tiles[slot].astype(jnp.float32), precision=lax.Precision.HIGHEST)
    return total.reshape(field.shape)

def horizontal_adjoint(field, tiles, picks):
    shaped = field.astype(jnp.float32).reshape(field.shape[:-1] + (NBLK, BLOCK))
    total = jnp.zeros(shaped.shape, jnp.float32)
    for slot in range(KNB):
        term = jnp.einsum('...bc,dc->...bd', shaped, tiles[slot].astype(jnp.float32), precision=lax.Precision.HIGHEST)
        total = total + jnp.einsum('bj,...bd->...jd', picks[slot], term, precision=lax.Precision.HIGHEST)
    return total.reshape(field.shape)

def to_blocks(field):
    shaped = field.reshape(V, N_MEM, LEVELS // N_MEM, N_LEV, COLS // N_LEV)
    return jnp.transpose(shaped, (3, 1, 0, 2, 4)).reshape(N_LEV * N_MEM, -1)

def from_blocks(blocks):
    shaped = blocks.reshape(N_LEV, N_MEM, V, LEVELS // N_MEM, COLS // N_LEV)
    return jnp.transpose(shaped, (2, 1, 3, 0, 4)).reshape(V, LEVELS, COLS)

def scatter_row(zeros_row, where_at, values):
    return zeros_row.at[where_at].add(values)

def reference(control, static_control_vector, perturb, tiles, block_offset, vert, static_vertical_root, obs_index, obs_value, obs_sigma, huber_mask):
    picks = selectors(block_offset)
    ens_gain = ENS_W / math.sqrt(M)
    weights = jnp.where(huber_mask == 1, jnp.float32(1.0), jnp.float32(HUBER_LOW))
    precision_obs = (weights / (obs_sigma * obs_sigma)).reshape(N_LEV * N_MEM, -1)
    where_obs = obs_index.reshape(N_LEV * N_MEM, -1).astype(jnp.int32)
    values_obs = obs_value.reshape(N_LEV * N_MEM, -1)
    vertical_forward = vert.astype(jnp.float32)
    static_forward = static_vertical_root.astype(jnp.float32)
    for turn in range(ITERS):
        local = lax.map(lambda member: horizontal(member, tiles, picks).astype(jnp.bfloat16), control)

        def accumulate(carry, pair):
            member_localized, member_pert = pair
            column_slice = jnp.einsum('tbu,tuo->tbo', vertical_forward, member_localized.astype(jnp.float32), precision=lax.Precision.HIGHEST)
            return (carry + column_slice * member_pert.astype(jnp.float32), None)
        ens, _ = lax.scan(accumulate, jnp.zeros((V, LEVELS, COLS), jnp.float32), (local, perturb))
        static_portion = jnp.einsum('tbu,tuo->tbo', static_forward, static_control_vector.astype(jnp.float32), precision=lax.Precision.HIGHEST)
        increment = ens_gain * ens + STATIC_WEIGHT * static_portion
        blocks = to_blocks(increment)
        seen = jnp.take_along_axis(blocks, where_obs, axis=1)
        resid = precision_obs * (seen - values_obs)
        grad_blocks = jax.vmap(scatter_row)(jnp.zeros_like(blocks), where_obs, resid)
        gradient_field_total = from_blocks(grad_blocks)
        static_gradient = static_control_vector.astype(jnp.float32) + STATIC_WEIGHT * jnp.einsum('otn,ote->one', static_forward, gradient_field_total, precision=lax.Precision.HIGHEST)

        def update(pair):
            member_ctl, member_pert = pair
            weighted_innovations = ens_gain * gradient_field_total * member_pert.astype(jnp.float32)
            backward_field = jnp.einsum('otn,ote->one', vertical_forward, weighted_innovations, precision=lax.Precision.HIGHEST).astype(jnp.bfloat16)
            adjoint = horizontal_adjoint(backward_field, tiles, picks)
            current = member_ctl.astype(jnp.float32)
            return (current - TAU * (current + adjoint)).astype(jnp.bfloat16)
        control = lax.map(update, (control, perturb))
        static_control_vector = (static_control_vector.astype(jnp.float32) - TAU * static_gradient).astype(jnp.bfloat16)
    return (control, static_control_vector)
```

```python
import functools
import math

import jax
import jax.numpy as jnp
from jax import lax
from jax.experimental import pallas as pl
from jax.experimental.pallas import tpu as pltpu
from jax.sharding import PartitionSpec as P

ITERS = 2

ENS_W = 0.85
STATIC_WEIGHT = 0.5
TAU = 0.5
HUBER_LOW = 0.3

F32 = jnp.float32
BF16 = jnp.bfloat16
LANES = 128
HALF = 64


def call(body, out_shape, scratch=()):
    return pl.pallas_call(body, out_shape=out_shape, scratch_shapes=list(scratch), name=body.__name__)


def dot(a, b, dims=((1,), (0,))):
    return lax.dot_general(a, b, (dims, ((), ())), preferred_element_type=F32)


def spread(load, pick_ref, weight_ref, gathered):
    rows = gathered.shape[0] // 32
    lane = lax.broadcasted_iota(jnp.int32, (32, LANES), 1)
    pick = pick_ref[...]
    for first in range(0, rows, 2):
        columns = []
        for r in (first, first + 1):
            x = load(r)
            low = jnp.where(lane < HALF, x, 0.0)
            columns.append(jnp.concatenate([low, x - low], axis=0).astype(BF16))
        moved = dot(pick, jnp.concatenate(columns, axis=1)).astype(BF16)
        for i in range(2):
            for a in range(8):
                gathered[pl.ds((first + i) * 32, 32), pl.ds(a * LANES, LANES)] = moved[
                    a * 32 : a * 32 + 32, i * LANES : (i + 1) * LANES
                ]
    return dot(gathered[...], weight_ref[...])


def open_chunks(recv_ref, scratch):
    rows = recv_ref.shape[1]
    for j in range(recv_ref.shape[0]):
        scratch[pl.ds(j * rows, rows), :] = recv_ref[j].astype(F32)


def close_chunks(scratch, send_ref):
    rows = send_ref.shape[1]
    for j in range(send_ref.shape[0]):
        send_ref[j] = scratch[pl.ds(j * rows, rows), :].astype(BF16)


def forward_first(control_ref, pick_ref, weight_ref, send_ref, kept_ref, flat, gathered):
    members, variables, levels, columns = control_ref.shape
    rows = members * variables * levels
    for m in range(members):
        for v in range(variables):
            x = control_ref[m, v].astype(F32)
            for j in range(columns // LANES):
                flat[pl.ds(j * rows + (m * variables + v) * levels, levels), :] = x[:, j * LANES : (j + 1) * LANES]

    def load(r):
        x = flat[pl.ds(r, 32, stride=rows), :]
        kept_ref[r] = x.astype(BF16)
        return x

    local = spread(load, pick_ref, weight_ref, gathered)
    for r in range(rows):
        flat[pl.ds(r, 32, stride=rows), :] = local[r * 32 : r * 32 + 32]
    close_chunks(flat, send_ref)


def descend(recv_ref, kept_ref, pick_ref, weight_ref, flat, gathered):
    rows = recv_ref.shape[1]
    open_chunks(recv_ref, flat)
    adjoint = spread(lambda r: flat[pl.ds(r, 32, stride=rows), :], pick_ref, weight_ref, gathered)
    current = kept_ref[...].astype(F32).reshape(rows * 32, LANES)
    return current - TAU * (current + adjoint)


def backward_forward(
    recv_ref, kept_ref, pick_t_ref, weight_t_ref, pick_ref, weight_ref, send_ref, next_ref, flat, gathered
):
    rows = recv_ref.shape[1]
    updated = descend(recv_ref, kept_ref, pick_t_ref, weight_t_ref, flat, gathered).astype(BF16)
    next_ref[...] = updated.reshape(rows, 32, LANES)
    local = spread(lambda r: next_ref[r].astype(F32), pick_ref, weight_ref, gathered)
    for r in range(rows):
        flat[pl.ds(r, 32, stride=rows), :] = local[r * 32 : r * 32 + 32]
    close_chunks(flat, send_ref)


def backward_last(recv_ref, kept_ref, pick_t_ref, weight_t_ref, control_ref, flat, gathered):
    members, variables, levels, columns = control_ref.shape
    flat[...] = descend(recv_ref, kept_ref, pick_t_ref, weight_t_ref, flat, gathered)
    for m in range(members):
        for v in range(variables):
            start = (m * variables + v) * levels * 32
            for j in range(columns // LANES):
                control_ref[m, v, :, pl.ds(j * LANES, LANES)] = flat[pl.ds(start + j, levels, stride=32), :].astype(
                    BF16
                )


def ensemble(recv_ref, perturb_ref, vert_ref, send_ref, flat):
    members, variables = perturb_ref.shape[:2]
    rows = recv_ref.shape[1]
    levels = rows // (members * variables)
    open_chunks(recv_ref, flat)
    totals = []
    for v in range(variables):
        total = None
        for m in range(members):
            start = (m * variables + v) * levels
            x = jnp.concatenate([flat[pl.ds(start + i, 32, stride=rows), :] for i in range(levels)], axis=0)
            term = dot(vert_ref[v], x.astype(BF16), ((0,), (0,))) * perturb_ref[m, v].astype(F32)
            total = term if total is None else total + term
        totals.append(total)
    deep = send_ref.shape[1] // variables
    for d in range(send_ref.shape[0]):
        send_ref[d] = jnp.concatenate([t[d * deep : (d + 1) * deep] for t in totals], axis=0).astype(send_ref.dtype)


def observations(index_ref, value_ref, sigma_ref, mask_ref, slope_ref, shift_ref):
    cells = slope_ref.shape[0]
    weights = jnp.where(mask_ref[...] == 1, F32(1.0), F32(HUBER_LOW))
    precision = weights / (sigma_ref[...] * sigma_ref[...])
    pulled = precision * value_ref[...]
    index = index_ref[...]
    lefts, rights = [], []
    for o in range(index.shape[0]):
        at = index[o : o + 1]
        row = lax.broadcasted_iota(jnp.int32, (cells, LANES), 0) == at // LANES
        lane = lax.broadcasted_iota(jnp.int32, (LANES, LANES), 0) == at % LANES
        lefts.append(
            jnp.concatenate(
                [jnp.where(row, precision[o : o + 1], 0.0), jnp.where(row, pulled[o : o + 1], 0.0)], axis=0
            )
        )
        rights.append(jnp.where(lane, F32(1.0), F32(0.0)))
    both = lax.dot_general(
        jnp.concatenate(lefts, axis=1),
        jnp.concatenate(rights, axis=1),
        (((1,), (1,)), ((), ())),
        precision=lax.Precision.HIGHEST,
        preferred_element_type=F32,
    )
    slope_ref[...] = both[:cells]
    shift_ref[...] = both[cells:]


def gradient(gain, recv_ref, static_ref, root_ref, slope_ref, shift_ref, send_ref):
    ens = jnp.sum(recv_ref[...].astype(F32), axis=0)
    static = jnp.concatenate([dot(root_ref[v], static_ref[v]) for v in range(static_ref.shape[0])], axis=0)
    increment = gain * ens + STATIC_WEIGHT * static
    grad = (slope_ref[...] * increment - shift_ref[...]).astype(send_ref.dtype)
    for d in range(send_ref.shape[0]):
        send_ref[d] = grad


def backward(gain, recv_ref, perturb_ref, vert_ref, root_ref, static_ref, send_ref, next_ref, flat):
    members, variables, levels_all = perturb_ref.shape[:3]
    rows = send_ref.shape[1]
    levels = rows // (members * variables)
    deep = recv_ref.shape[1] // variables
    field = recv_ref[...].astype(F32)
    for v in range(variables):
        grad = field[:, v * deep : (v + 1) * deep, :].reshape(levels_all, LANES)
        for m in range(members):
            weighted = ((gain * grad) * perturb_ref[m, v].astype(F32)).astype(BF16)
            back = dot(vert_ref[v], weighted)
            start = (m * variables + v) * levels
            for i in range(levels):
                flat[pl.ds(start + i, 32, stride=rows), :] = back[i * 32 : i * 32 + 32]
        current = static_ref[v].astype(F32)
        slope = current + STATIC_WEIGHT * dot(root_ref[v], grad.astype(BF16), ((0,), (0,)))
        next_ref[v] = (current - TAU * slope).astype(BF16)
    close_chunks(flat, send_ref)


def tables(block_offset):
    count, slots = block_offset.shape
    blocks = jnp.arange(count, dtype=jnp.int32)
    source = (blocks[:, None] + block_offset) % count
    spot = (source % 2) * (count // 2) + source // 2
    by_slot = spot.reshape(count // 2, 2, slots).transpose(2, 1, 0)
    place = jnp.arange(count, dtype=jnp.int32)
    forth = by_slot.reshape(-1, 1) == place[None, :]
    back = (by_slot.reshape(slots, 1, count) == place[None, :, None]).reshape(slots * count, count)
    return forth.astype(BF16), back.astype(BF16)


def weights(tiles):
    slots, width = tiles.shape[:2]
    left = jnp.pad(tiles, ((0, 0), (0, 0), (0, width)))
    right = jnp.pad(tiles, ((0, 0), (0, 0), (width, 0)))
    both = jnp.stack([left, left, right, right], axis=1)
    return both.reshape(slots * 4 * width, 2 * width)


def on_device(
    control,
    static_control_vector,
    perturb,
    tiles,
    block_offset,
    vert,
    static_vertical_root,
    obs_index,
    obs_value,
    obs_sigma,
    huber_mask,
):
    n_lev, n_mem = lax.axis_size("lev"), lax.axis_size("mem")
    members, variables, levels, columns = control.shape
    levels_all = vert.shape[1]
    deep = levels_all // n_mem
    rows, cells = members * variables * levels, variables * deep
    gain = ENS_W / math.sqrt(members * n_mem)

    pick, pick_t = tables(block_offset)
    weight, weight_t = weights(tiles), weights(jnp.swapaxes(tiles, 1, 2))
    turned = vert.reshape(variables, levels_all, n_lev, levels).transpose(0, 3, 2, 1).reshape(vert.shape)
    own_root = lax.dynamic_slice_in_dim(static_vertical_root, lax.axis_index("mem") * deep, deep, 1)

    shape = jax.ShapeDtypeStruct
    chunks = shape((n_lev, rows, LANES), BF16)
    kept = shape((rows, n_lev, LANES), BF16)
    parts = shape((n_mem, cells, LANES), BF16)
    flat = pltpu.VMEM((n_lev * rows, LANES), F32)
    gathered = pltpu.VMEM((n_lev * rows, 8 * LANES), BF16)
    field = shape((cells, LANES), F32)

    flat_obs = lambda x: x.reshape(-1, LANES)
    slope, shift = call(observations, (field, field))(
        flat_obs(obs_index), flat_obs(obs_value), flat_obs(obs_sigma), flat_obs(huber_mask)
    )
    across = lambda x, axis: lax.all_to_all(x, axis, 0, 0, tiled=True)

    send, held = call(forward_first, (chunks, kept), (flat, gathered))(control, pick, weight)
    static = static_control_vector
    for turn in range(ITERS):
        partial = call(ensemble, parts, (flat,))(across(send, "lev"), perturb, turned)
        grad_call = functools.partial(gradient, gain)
        grad_call.__name__ = "gradient"
        grad = call(grad_call, parts)(across(partial, "mem"), static, own_root, slope, shift)
        back_call = functools.partial(backward, gain)
        back_call.__name__ = "backward"
        send, static = call(back_call, (chunks, shape(static.shape, BF16)), (flat,))(
            across(grad, "mem"), perturb, turned, static_vertical_root, static
        )
        levels_back = across(send, "lev")
        if turn + 1 < ITERS:
            send, held = call(backward_forward, (chunks, kept), (flat, gathered))(
                levels_back, held, pick_t, weight_t, pick, weight
            )
        else:
            control = call(backward_last, shape(control.shape, BF16), (flat, gathered))(
                levels_back, held, pick_t, weight_t
            )
    return (control, static)


def solution(mesh):
    placed = (
        P("mem", None, "lev", None),
        P(None, None, "lev"),
        P("mem", None, None, "lev"),
        P(),
        P(),
        P(),
        P(),
        P(("lev", "mem")),
        P(("lev", "mem")),
        P(("lev", "mem")),
        P(("lev", "mem")),
    )
    return jax.shard_map(
        on_device,
        mesh=mesh,
        in_specs=placed,
        out_specs=(P("mem", None, "lev", None), P(None, None, "lev")),
        check_vma=False,
    )
```

```python
import functools
import math

import jax
import jax.numpy as jnp
from jax import lax
from jax.experimental import pallas as pl
from jax.experimental.pallas import tpu as pltpu
from jax.sharding import PartitionSpec as P

ITERS = 2

ENS_W = 0.85
STATIC_WEIGHT = 0.5
TAU = 0.5
HUBER_LOW = 0.3

F32 = jnp.float32
BF16 = jnp.bfloat16
LANES = 128
HALF = 64
SPANS = ((0, 5),)


def call(body, out_shape, scratch=(), *static):
    bound = functools.partial(body, *static)
    run = pl.pallas_call(bound, out_shape=out_shape, scratch_shapes=list(scratch), name=body.__name__)
    return lambda *args: run(*(pltpu.with_memory_space_constraint(a, pltpu.VMEM) for a in args))


def dot(a, b, dims=((1,), (0,))):
    return lax.dot_general(a, b, (dims, ((), ())), preferred_element_type=F32)


def spread(load, pick_ref, weight_ref, gathered):
    rows = gathered.shape[0] // 32
    lane = lax.broadcasted_iota(jnp.int32, (32, LANES), 1)
    pick = pick_ref[...]
    for first in range(0, rows, 2):
        columns = []
        for r in (first, first + 1):
            x = load(r)
            low = jnp.where(lane < HALF, x, 0.0)
            columns.append(jnp.concatenate([low, x - low], axis=0).astype(BF16))
        moved = dot(pick, jnp.concatenate(columns, axis=1)).astype(BF16)
        for i in range(2):
            for a in range(8):
                gathered[pl.ds((first + i) * 32, 32), pl.ds(a * LANES, LANES)] = moved[
                    a * 32 : a * 32 + 32, i * LANES : (i + 1) * LANES
                ]
    return dot(gathered[...], weight_ref[...])


def open_chunks(recv_ref, flat):
    rows = recv_ref.shape[1]
    for j in range(recv_ref.shape[0]):
        flat[pl.ds(j * rows, rows), :] = recv_ref[j].astype(F32)


def close_chunks(flat, send_ref):
    rows = send_ref.shape[1]
    for j in range(send_ref.shape[0]):
        send_ref[j] = flat[pl.ds(j * rows, rows), :].astype(BF16)


def by_row(flat, r, rows):
    return flat.at[pl.ds(r, 32, stride=rows), :]


def send_local(local, flat, send_ref):
    rows = send_ref.shape[1]
    for r in range(rows):
        by_row(flat, r, rows)[...] = local[r * 32 : r * 32 + 32]
    close_chunks(flat, send_ref)


def forward_first(span, control_ref, pick_ref, weight_ref, send_ref, kept_ref, flat, gathered):
    members, _, levels, columns = control_ref.shape
    rows = send_ref.shape[1]
    at = 0
    for m in range(members):
        for v in range(*span):
            x = control_ref[m, v].astype(F32)
            for j in range(columns // LANES):
                flat[pl.ds(j * rows + at, levels), :] = x[:, j * LANES : (j + 1) * LANES]
            at += levels

    def load(r):
        x = by_row(flat, r, rows)[...]
        kept_ref[r] = x.astype(BF16)
        return x

    send_local(spread(load, pick_ref, weight_ref, gathered), flat, send_ref)


def descend(recv_ref, kept_ref, pick_ref, weight_ref, flat, gathered):
    rows = recv_ref.shape[1]
    open_chunks(recv_ref, flat)
    adjoint = spread(lambda r: by_row(flat, r, rows)[...], pick_ref, weight_ref, gathered)
    current = kept_ref[...].astype(F32).reshape(rows * 32, LANES)
    return current - TAU * (current + adjoint)


def backward_forward(
    recv_ref, kept_ref, pick_t_ref, weight_t_ref, pick_ref, weight_ref, send_ref, next_ref, flat, gathered
):
    rows = recv_ref.shape[1]
    updated = descend(recv_ref, kept_ref, pick_t_ref, weight_t_ref, flat, gathered).astype(BF16)
    next_ref[...] = updated.reshape(rows, 32, LANES)
    local = spread(lambda r: next_ref[r].astype(F32), pick_ref, weight_ref, gathered)
    send_local(local, flat, send_ref)


def backward_last(spans, *refs):
    n = len(spans)
    recvs, helds = refs[:n], refs[n : 2 * n]
    pick_t_ref, weight_t_ref, control_ref = refs[2 * n : 2 * n + 3]
    scratch = refs[2 * n + 3 :]
    members, _, levels, columns = control_ref.shape
    for c, span in enumerate(spans):
        flat, gathered = scratch[2 * c], scratch[2 * c + 1]
        flat[...] = descend(recvs[c], helds[c], pick_t_ref, weight_t_ref, flat, gathered)
        start = 0
        for m in range(members):
            for v in range(*span):
                for j in range(columns // LANES):
                    x = flat[pl.ds(start + j, levels, stride=32), :]
                    control_ref[m, v, :, pl.ds(j * LANES, LANES)] = x.astype(BF16)
                start += levels * 32


def ensemble(span, recv_ref, perturb_ref, vert_ref, send_ref, flat):
    members = perturb_ref.shape[0]
    rows = recv_ref.shape[1]
    count = span[1] - span[0]
    levels = rows // (members * count)
    open_chunks(recv_ref, flat)
    totals = []
    for v in range(count):
        total = None
        for m in range(members):
            start = (m * count + v) * levels
            x = jnp.concatenate([by_row(flat, start + i, rows)[...] for i in range(levels)], axis=0)
            term = dot(vert_ref[span[0] + v], x.astype(BF16), ((0,), (0,)))
            term = term * perturb_ref[m, span[0] + v].astype(F32)
            total = term if total is None else total + term
        totals.append(total)
    deep = send_ref.shape[1] // count
    for d in range(send_ref.shape[0]):
        send_ref[d] = jnp.concatenate([t[d * deep : (d + 1) * deep] for t in totals], axis=0).astype(send_ref.dtype)


def observations(index_ref, value_ref, sigma_ref, mask_ref, slope_ref, shift_ref):
    cells = slope_ref.shape[0]
    weights = jnp.where(mask_ref[...] == 1, F32(1.0), F32(HUBER_LOW))
    precision = weights / (sigma_ref[...] * sigma_ref[...])
    pulled = precision * value_ref[...]
    index = index_ref[...]
    lefts, rights = [], []
    for o in range(index.shape[0]):
        at = index[o : o + 1]
        row = lax.broadcasted_iota(jnp.int32, (cells, LANES), 0) == at // LANES
        lane = lax.broadcasted_iota(jnp.int32, (LANES, LANES), 0) == at % LANES
        lefts.append(
            jnp.concatenate(
                [jnp.where(row, precision[o : o + 1], 0.0), jnp.where(row, pulled[o : o + 1], 0.0)], axis=0
            )
        )
        rights.append(jnp.where(lane, F32(1.0), F32(0.0)))
    both = lax.dot_general(
        jnp.concatenate(lefts, axis=1),
        jnp.concatenate(rights, axis=1),
        (((1,), (1,)), ((), ())),
        precision=lax.Precision.HIGHEST,
        preferred_element_type=F32,
    )
    slope_ref[...] = both[:cells]
    shift_ref[...] = both[cells:]


def gradient(gain, span, offset, recv_ref, static_ref, root_ref, slope_ref, shift_ref, send_ref):
    cells = recv_ref.shape[1]
    count = span[1] - span[0]
    deep = cells // count
    ens = jnp.sum(recv_ref[...].astype(F32), axis=0)
    static = jnp.concatenate([dot(root_ref[span[0] + v], static_ref[offset + v]) for v in range(count)], axis=0)
    increment = gain * ens + STATIC_WEIGHT * static
    own = pl.ds(span[0] * deep, cells)
    grad = (slope_ref[own, :] * increment - shift_ref[own, :]).astype(send_ref.dtype)
    for d in range(send_ref.shape[0]):
        send_ref[d] = grad


def backward(gain, span, offset, recv_ref, perturb_ref, vert_ref, root_ref, static_ref, send_ref, next_ref, flat):
    members, _, levels_all = perturb_ref.shape[:3]
    rows = send_ref.shape[1]
    count = span[1] - span[0]
    levels = rows // (members * count)
    deep = recv_ref.shape[1] // count
    field = recv_ref[...].astype(F32)
    for v in range(count):
        grad = field[:, v * deep : (v + 1) * deep, :].reshape(levels_all, LANES)
        for m in range(members):
            weighted = (gain * grad) * perturb_ref[m, span[0] + v].astype(F32)
            high = weighted.astype(BF16)
            low = (weighted - high.astype(F32)).astype(BF16)
            back = dot(vert_ref[span[0] + v], high) + dot(vert_ref[span[0] + v], low)
            start = (m * count + v) * levels
            for i in range(levels):
                by_row(flat, start + i, rows)[...] = back[i * 32 : i * 32 + 32]
        current = static_ref[offset + v].astype(F32)
        slope = current + STATIC_WEIGHT * dot(root_ref[span[0] + v], grad.astype(BF16), ((0,), (0,)))
        next_ref[v] = (current - TAU * slope).astype(BF16)
    close_chunks(flat, send_ref)


def tables(block_offset):
    count, slots = block_offset.shape
    blocks = jnp.arange(count, dtype=jnp.int32)
    source = (blocks[:, None] + block_offset) % count
    spot = (source % 2) * (count // 2) + source // 2
    by_slot = spot.reshape(count // 2, 2, slots).transpose(2, 1, 0)
    place = jnp.arange(count, dtype=jnp.int32)
    forth = by_slot.reshape(-1, 1) == place[None, :]
    back = (by_slot.reshape(slots, 1, count) == place[None, :, None]).reshape(slots * count, count)
    return forth.astype(BF16), back.astype(BF16)


def weights(tiles):
    slots, width = tiles.shape[:2]
    left = jnp.pad(tiles, ((0, 0), (0, 0), (0, width)))
    right = jnp.pad(tiles, ((0, 0), (0, 0), (width, 0)))
    both = jnp.stack([left, left, right, right], axis=1)
    return both.reshape(slots * 4 * width, 2 * width)


def on_device(
    control,
    static_control_vector,
    perturb,
    tiles,
    block_offset,
    vert,
    static_vertical_root,
    obs_index,
    obs_value,
    obs_sigma,
    huber_mask,
):
    n_lev, n_mem = lax.axis_size("lev"), lax.axis_size("mem")
    members, variables, levels, columns = control.shape
    levels_all = vert.shape[1]
    deep = levels_all // n_mem
    gain = ENS_W / math.sqrt(members * n_mem)

    pick, pick_t = tables(block_offset)
    weight, weight_t = weights(tiles), weights(jnp.swapaxes(tiles, 1, 2))
    turned = vert.reshape(variables, levels_all, n_lev, levels).transpose(0, 3, 2, 1).reshape(vert.shape)
    own_root = lax.dynamic_slice_in_dim(static_vertical_root, lax.axis_index("mem") * deep, deep, 1)

    shape = pltpu.VMEM
    field = shape((variables * deep, LANES), F32)
    flat_obs = lambda x: x.reshape(-1, LANES)
    across = lambda x, axis: lax.all_to_all(x, axis, 0, 0, tiled=True)

    rows = [members * (b - a) * levels for a, b in SPANS]
    chunks = [shape((n_lev, r, LANES), BF16) for r in rows]
    kept = [shape((r, n_lev, LANES), BF16) for r in rows]
    parts = [shape((n_mem, (b - a) * deep, LANES), BF16) for a, b in SPANS]
    statics = [shape((b - a, *static_control_vector.shape[1:]), BF16) for a, b in SPANS]
    flat = [pltpu.VMEM((n_lev * r, LANES), F32) for r in rows]
    both = [(f, pltpu.VMEM((n_lev * r, 8 * LANES), BF16)) for f, r in zip(flat, rows)]
    every = range(len(SPANS))

    send, held = [None] * len(SPANS), [None] * len(SPANS)
    static = [static_control_vector] * len(SPANS)
    offset = [a for a, _ in SPANS]
    for c in every:
        send[c], held[c] = call(forward_first, (chunks[c], kept[c]), both[c], SPANS[c])(control, pick, weight)
        send[c] = across(send[c], "lev")
    slope, shift = call(observations, (field, field))(
        flat_obs(obs_index), flat_obs(obs_value), flat_obs(obs_sigma), flat_obs(huber_mask)
    )
    for turn in range(ITERS):
        for c in every:
            send[c] = call(ensemble, parts[c], flat[c : c + 1], SPANS[c])(send[c], perturb, turned)
            send[c] = across(send[c], "mem")
        for c in every:
            send[c] = call(gradient, parts[c], (), gain, SPANS[c], offset[c])(
                send[c], static[c], own_root, slope, shift
            )
            send[c] = across(send[c], "mem")
        for c in every:
            send[c], static[c] = call(backward, (chunks[c], statics[c]), flat[c : c + 1], gain, SPANS[c], offset[c])(
                send[c], perturb, turned, static_vertical_root, static[c]
            )
            offset[c] = 0
            send[c] = across(send[c], "lev")
        for c in every:
            if turn + 1 < ITERS:
                send[c], held[c] = call(backward_forward, (chunks[c], kept[c]), both[c])(
                    send[c], held[c], pick_t, weight_t, pick, weight
                )
                send[c] = across(send[c], "lev")
    scratch = [buffer for pair in both for buffer in pair]
    control = call(backward_last, shape(control.shape, BF16), scratch, SPANS)(*send, *held, pick_t, weight_t)
    return (control, jnp.concatenate(static, axis=0))


def solution(mesh):
    placed = (
        P("mem", None, "lev", None),
        P(None, None, "lev"),
        P("mem", None, None, "lev"),
        P(),
        P(),
        P(),
        P(),
        P(("lev", "mem")),
        P(("lev", "mem")),
        P(("lev", "mem")),
        P(("lev", "mem")),
    )
    return jax.shard_map(
        on_device,
        mesh=mesh,
        in_specs=placed,
        out_specs=(P("mem", None, "lev", None), P(None, None, "lev")),
        check_vma=False,
    )
```

```python
import functools
import math

import jax
import jax.numpy as jnp
from jax import lax
from jax.experimental import pallas as pl
from jax.experimental.pallas import tpu as pltpu
from jax.sharding import PartitionSpec as P

ITERS = 2

ENS_W = 0.85
STATIC_WEIGHT = 0.5
TAU = 0.5
HUBER_LOW = 0.3

F32 = jnp.float32
BF16 = jnp.bfloat16
LANES = 128
HALF = 64
PAIRS = 32
BLOCKS = 64
GROUP = 5


def call(body, out_shape, scratch, args, stay=(), **static):
    run = pl.pallas_call(
        functools.partial(body, **static),
        out_shape=out_shape,
        in_specs=[pl.BlockSpec(memory_space=pl.ANY if i in stay else pltpu.VMEM) for i in range(len(args))],
        scratch_shapes=list(scratch),
        name=body.__name__,
    )
    return run(*(a if i in stay else pltpu.with_memory_space_constraint(a, pltpu.VMEM) for i, a in enumerate(args)))


def dot(a, b, dims=((1,), (0,))):
    return lax.dot_general(a, b, (dims, ((), ())), preferred_element_type=F32)


def iota(shape, axis):
    return lax.broadcasted_iota(jnp.int32, shape, axis)


def ones(mask):
    return jnp.where(mask, F32(1.0), F32(0.0)).astype(BF16)


def swap_halves(x, y):
    low = iota(x.shape, 1) < HALF
    first = jnp.where(low, x, pltpu.roll(y, HALF, 1))
    second = jnp.where(low, pltpu.roll(x, HALF, 1), y)
    return first, second


def spread(load, store, pick_ref, weight_ref, moved_ref):
    count = moved_ref.shape[0] // BLOCKS
    pick = pick_ref[...]
    for g in range(0, count, GROUP):
        group = [jnp.concatenate(swap_halves(load(2 * p), load(2 * p + 1)), axis=0) for p in range(g, g + GROUP)]
        moved = dot(pick, jnp.concatenate(group, axis=1).astype(BF16)).astype(BF16)
        for i in range(GROUP):
            for k in range(pick.shape[0] // BLOCKS):
                moved_ref[pl.ds((g + i) * BLOCKS, BLOCKS), pl.ds(k * LANES, LANES)] = moved[
                    k * BLOCKS : (k + 1) * BLOCKS, i * LANES : (i + 1) * LANES
                ]
        out = dot(moved_ref[pl.ds(g * BLOCKS, GROUP * BLOCKS), :], weight_ref[...])
        for p in range(GROUP):
            at = p * BLOCKS
            x, y = swap_halves(out[at : at + PAIRS], out[at + PAIRS : at + BLOCKS])
            store(2 * (g + p), x)
            store(2 * (g + p) + 1, y)


def open_chunks(recv_ref, flat):
    rows = recv_ref.shape[1]
    for j in range(recv_ref.shape[0]):
        flat[pl.ds(j * rows, rows), :] = recv_ref[j].astype(F32)


def close_chunks(flat, send_ref):
    rows = send_ref.shape[1]
    for j in range(send_ref.shape[0]):
        send_ref[j] = flat[pl.ds(j * rows, rows), :].astype(BF16)


def by_row(flat, rows):
    at = lambda r: pl.ds(r, PAIRS, stride=rows)

    def load(r):
        return flat[at(r), :]

    def store(r, x):
        flat[at(r), :] = x

    return load, store


def forward_first(
    control_hbm,
    offset_hbm,
    tiles_hbm,
    send_ref,
    kept_hbm,
    flat,
    moved,
    pick,
    weight,
    kept,
    control,
    offset_ref,
    tiles_ref,
    sems,
):
    members, variables, levels, columns = control.shape
    rows = send_ref.shape[1]
    fetch = [pltpu.make_async_copy(control_hbm.at[m], control.at[m], sems.at[m]) for m in range(members)]
    small = [
        pltpu.make_async_copy(offset_hbm, offset_ref, sems.at[members + 1]),
        pltpu.make_async_copy(tiles_hbm, tiles_ref, sems.at[members + 2]),
    ]
    for copy in small + fetch:
        copy.start()
    for copy in small:
        copy.wait()
    square = (BLOCKS, BLOCKS)
    block = iota(square, 1)
    turn = ones(iota(square, 0) == (block & 1) * PAIRS + (block >> 1))
    wide = (HALF, LANES)
    left, right = ones(iota(wide, 1) == iota(wide, 0)), ones(iota(wide, 1) == iota(wide, 0) + HALF)
    for k in range(tiles_ref.shape[0]):
        source = (block[:1] + offset_ref[k : k + 1, :]) & (BLOCKS - 1)
        spot = (source & 1) * PAIRS + (source >> 1)
        found = ones(iota(square, 0) == spot)
        pick[pl.ds(k * BLOCKS, BLOCKS), :] = dot(turn, found, ((1,), (1,))).astype(BF16)
        tile = tiles_ref[k]
        weight[pl.ds(2 * k * HALF, HALF), :] = dot(tile, left).astype(BF16)
        weight[pl.ds((2 * k + 1) * HALF, HALF), :] = dot(tile, right).astype(BF16)
    for m in range(members):
        fetch[m].wait()
        for v in range(variables):
            x = control[m, v].astype(F32)
            at = (m * variables + v) * levels
            for j in range(columns // LANES):
                flat[pl.ds(j * rows + at, levels), :] = x[:, j * LANES : (j + 1) * LANES]

    load, store = by_row(flat, rows)

    def load_kept(r):
        x = load(r)
        kept[r] = x.astype(BF16)
        return x

    keep = pltpu.make_async_copy(kept, kept_hbm, sems.at[members])
    spread(load_kept, store, pick, weight, moved)
    keep.start()
    close_chunks(flat, send_ref)
    keep.wait()


def by_variable(recv_ref, variables):
    deep = recv_ref.shape[1] // variables
    field = recv_ref[...].astype(F32)
    return [field[:, v * deep : (v + 1) * deep, :].reshape(-1, LANES) for v in range(variables)]


def descend_static(grad_ref, root_ref, static_ref, next_ref):
    for v, grad in enumerate(by_variable(grad_ref, static_ref.shape[0])):
        current = static_ref[v].astype(F32)
        slope = current + STATIC_WEIGHT * dot(root_ref[v], grad.astype(BF16))
        next_ref[v] = (current - TAU * slope).astype(BF16)


def backward_forward(
    recv_ref,
    kept_ref,
    pick_t_ref,
    weight_t_ref,
    grad_ref,
    root_ref,
    static_ref,
    pick_ref,
    weight_ref,
    send_ref,
    next_hbm,
    moving_hbm,
    flat,
    moved,
    next_ref,
    moving_ref,
    sems,
):
    descend_static(grad_ref, root_ref, static_ref, moving_ref)
    keep_static = pltpu.make_async_copy(moving_ref, moving_hbm, sems.at[0])
    keep_static.start()
    load, store = by_row(flat, recv_ref.shape[1])
    open_chunks(recv_ref, flat)

    def update(r, adjoint):
        current = kept_ref[r].astype(F32)
        next_ref[r] = (current - TAU * (current + adjoint)).astype(BF16)

    keep = pltpu.make_async_copy(next_ref, next_hbm, sems.at[1])
    spread(load, update, pick_t_ref, weight_t_ref, moved)
    keep.start()
    spread(lambda r: next_ref[r].astype(F32), store, pick_ref, weight_ref, moved)
    close_chunks(flat, send_ref)
    keep_static.wait()
    keep.wait()


def backward_last(
    recv_ref,
    kept_ref,
    pick_t_ref,
    weight_t_ref,
    grad_ref,
    root_ref,
    static_ref,
    control_hbm,
    moving_hbm,
    flat,
    moved,
    final,
    control,
    moving_ref,
    sems,
):
    members, variables, levels, columns = control.shape
    descend_static(grad_ref, root_ref, static_ref, moving_ref)
    keep_static = pltpu.make_async_copy(moving_ref, moving_hbm, sems.at[members])
    keep_static.start()
    load, _ = by_row(flat, recv_ref.shape[1])
    open_chunks(recv_ref, flat)

    def update(r, adjoint):
        current = kept_ref[r].astype(F32)
        final[pl.ds(r * PAIRS, PAIRS), :] = current - TAU * (current + adjoint)

    spread(load, update, pick_t_ref, weight_t_ref, moved)
    copies = [pltpu.make_async_copy(control.at[m], control_hbm.at[m], sems.at[m]) for m in range(members)]
    for m in range(members):
        for v in range(variables):
            start = (m * variables + v) * levels * PAIRS
            for j in range(columns // LANES):
                x = final[pl.ds(start + j, levels, stride=PAIRS), :]
                control[m, v, :, pl.ds(j * LANES, LANES)] = x.astype(BF16)
        copies[m].start()
    keep_static.wait()
    for copy in copies:
        copy.wait()


def ensemble(recv_ref, perturb_ref, vert_ref, send_ref, flat):
    members, variables = perturb_ref.shape[:2]
    rows = recv_ref.shape[1]
    levels = rows // (members * variables)
    load, _ = by_row(flat, rows)
    open_chunks(recv_ref, flat)
    totals = []
    for v in range(variables):
        total = None
        for m in range(members):
            start = (m * variables + v) * levels
            x = jnp.concatenate([load(start + i) for i in range(levels)], axis=0).astype(BF16)
            term = dot(vert_ref[v], x, ((0,), (0,))) * perturb_ref[m, v].astype(F32)
            total = term if total is None else total + term
        totals.append(total)
    deep = send_ref.shape[1] // variables
    for d in range(send_ref.shape[0]):
        send_ref[d] = jnp.concatenate([t[d * deep : (d + 1) * deep] for t in totals], axis=0).astype(send_ref.dtype)


def observations(index_ref, value_ref, sigma_ref, mask_ref, slope_ref, shift_ref):
    cells = slope_ref.shape[0]
    weights = jnp.where(mask_ref[...] == 1, F32(1.0), F32(HUBER_LOW))
    precision = weights / (sigma_ref[...] * sigma_ref[...])
    pulled = precision * value_ref[...]
    index = index_ref[...]
    lefts, rights = [], []
    for o in range(index.shape[0]):
        at = index[o : o + 1]
        row = iota((cells, LANES), 0) == at // LANES
        lane = iota((LANES, LANES), 0) == at % LANES
        lefts.append(
            jnp.concatenate(
                [jnp.where(row, precision[o : o + 1], 0.0), jnp.where(row, pulled[o : o + 1], 0.0)], axis=0
            )
        )
        rights.append(jnp.where(lane, F32(1.0), F32(0.0)))
    both = lax.dot_general(
        jnp.concatenate(lefts, axis=1),
        jnp.concatenate(rights, axis=1),
        (((1,), (1,)), ((), ())),
        precision=lax.Precision.HIGHEST,
        preferred_element_type=F32,
    )
    slope_ref[...] = both[:cells]
    shift_ref[...] = both[cells:]


def gradient(recv_ref, static_ref, root_ref, slope_ref, shift_ref, send_ref, *, gain):
    ens = jnp.sum(recv_ref[...].astype(F32), axis=0)
    static = jnp.concatenate([dot(root_ref[v], static_ref[v]) for v in range(static_ref.shape[0])], axis=0)
    increment = gain * ens + STATIC_WEIGHT * static
    grad = (slope_ref[...] * increment - shift_ref[...]).astype(send_ref.dtype)
    for d in range(send_ref.shape[0]):
        send_ref[d] = grad


def backward(recv_ref, perturb_ref, vert_ref, send_ref, flat, *, gain):
    members, variables = perturb_ref.shape[:2]
    rows = send_ref.shape[1]
    levels = rows // (members * variables)
    _, store = by_row(flat, rows)
    grads = by_variable(recv_ref, variables)
    for v in range(variables):
        for m in range(members):
            weighted = (gain * grads[v]) * perturb_ref[m, v].astype(F32)
            high = weighted.astype(BF16)
            low = (weighted - high.astype(F32)).astype(BF16)
            back = dot(vert_ref[v], high) + dot(vert_ref[v], low)
            start = (m * variables + v) * levels
            for i in range(levels):
                store(start + i, back[i * PAIRS : (i + 1) * PAIRS])
    close_chunks(flat, send_ref)


def tables(block_offset):
    count, slots = block_offset.shape
    blocks = jnp.arange(count, dtype=jnp.int32)
    source = (blocks[:, None] + block_offset) % count
    spot = (source % 2) * (count // 2) + source // 2
    by_slot = spot.reshape(count // 2, 2, slots).transpose(2, 1, 0)
    forth = by_slot.reshape(-1, 1) == blocks[None, :]
    back = (by_slot.reshape(slots, 1, count) == blocks[None, :, None]).reshape(slots * count, count)
    return forth.astype(BF16), back.astype(BF16)


def weights(tiles):
    slots, width = tiles.shape[:2]
    left = jnp.pad(tiles, ((0, 0), (0, 0), (0, width)))
    right = jnp.pad(tiles, ((0, 0), (0, 0), (width, 0)))
    return jnp.stack([left, right], axis=1).reshape(slots * 2 * width, 2 * width)


def on_device(
    control,
    static_control_vector,
    perturb,
    tiles,
    block_offset,
    vert,
    static_vertical_root,
    obs_index,
    obs_value,
    obs_sigma,
    huber_mask,
):
    n_lev, n_mem = lax.axis_size("lev"), lax.axis_size("mem")
    members, variables, levels, columns = control.shape
    levels_all = vert.shape[1]
    deep = levels_all // n_mem
    rows = members * variables * levels
    slots = tiles.shape[0]
    gain = ENS_W / math.sqrt(members * n_mem)

    pick, pick_t = tables(block_offset)
    weight, weight_t = weights(tiles), weights(jnp.swapaxes(tiles, 1, 2))
    turned = vert.reshape(variables, levels_all, n_lev, levels).transpose(0, 3, 2, 1).reshape(vert.shape)
    own_root = lax.dynamic_slice_in_dim(static_vertical_root, lax.axis_index("mem") * deep, deep, 1)

    vmem, hbm = pltpu.VMEM, pltpu.HBM
    chunks = vmem((n_lev, rows, LANES), BF16)
    parts = vmem((n_mem, variables * deep, LANES), BF16)
    field = vmem((variables * deep, LANES), F32)
    kept = (rows, PAIRS, LANES)
    flat = vmem((n_lev * rows, LANES), F32)
    moved = vmem((n_lev * rows, slots * LANES), BF16)
    dma = pltpu.SemaphoreType.DMA
    flat_obs = lambda x: x.reshape(-1, LANES)
    across = lambda x, axis: lax.all_to_all(x, axis, 0, 0, tiled=True)

    send, held = call(
        forward_first,
        (chunks, hbm(kept, BF16)),
        (
            flat,
            moved,
            vmem((slots * BLOCKS, BLOCKS), BF16),
            vmem((slots * LANES, LANES), BF16),
            vmem(kept, BF16),
            vmem(control.shape, BF16),
            vmem((slots, BLOCKS), jnp.int32),
            vmem(tiles.shape, BF16),
            dma((members + 3,)),
        ),
        (control, block_offset.T, tiles),
        stay=(0, 1, 2),
    )
    slope, shift = call(
        observations,
        (field, field),
        (),
        (flat_obs(obs_index), flat_obs(obs_value), flat_obs(obs_sigma), flat_obs(huber_mask)),
    )
    root_t = jnp.swapaxes(static_vertical_root, 1, 2)
    recv, slope, shift, own_root, root_t, turned, pick, pick_t, weight, weight_t = lax.optimization_barrier(
        (across(send, "lev"), slope, shift, own_root, root_t, turned, pick, pick_t, weight, weight_t)
    )
    static = static_control_vector
    for turn in range(ITERS):
        partial = call(ensemble, parts, (flat,), (recv, perturb, turned))
        grad = call(
            gradient, parts, (), (across(partial, "mem"), static, own_root, slope, shift), gain=gain
        )
        grad = across(grad, "mem")
        send = call(backward, chunks, (flat,), (grad, perturb, turned), gain=gain)
        operands = (across(send, "lev"), held, pick_t, weight_t, grad, root_t, static)
        if turn + 1 < ITERS:
            send, held, static = call(
                backward_forward,
                (chunks, hbm(kept, BF16), hbm(static.shape, BF16)),
                (flat, moved, vmem(kept, BF16), vmem(static.shape, BF16), dma((2,))),
                (*operands, pick, weight),
            )
            recv = across(send, "lev")
        else:
            control, static = call(
                backward_last,
                (hbm(control.shape, BF16), hbm(static.shape, BF16)),
                (
                    flat,
                    moved,
                    vmem((rows * PAIRS, LANES), F32),
                    vmem(control.shape, BF16),
                    vmem(static.shape, BF16),
                    dma((members + 1,)),
                ),
                operands,
            )
    return (control, static)


def solution(mesh):
    placed = (
        P("mem", None, "lev", None),
        P(None, None, "lev"),
        P("mem", None, None, "lev"),
        P(),
        P(),
        P(),
        P(),
        P(("lev", "mem")),
        P(("lev", "mem")),
        P(("lev", "mem")),
        P(("lev", "mem")),
    )
    return jax.shard_map(
        on_device,
        mesh=mesh,
        in_specs=placed,
        out_specs=(P("mem", None, "lev", None), P(None, None, "lev")),
        check_vma=False,
    )
```

```python
import functools
import math

import jax
import jax.numpy as jnp
from jax import lax
from jax.experimental import pallas as pl
from jax.experimental.pallas import tpu as pltpu
from jax.sharding import PartitionSpec as P

ITERS = 2

ENS_W = 0.85
STATIC_WEIGHT = 0.5
TAU = 0.5
HUBER_LOW = 0.3

F32 = jnp.float32
BF16 = jnp.bfloat16
LANES = 128
HALF = 64
PAIRS = 32
BLOCKS = 64
GROUP = 5


def call(body, out_shape, scratch, args, stay=(), **static):
    run = pl.pallas_call(
        functools.partial(body, **static),
        out_shape=out_shape,
        in_specs=[pl.BlockSpec(memory_space=pl.ANY if i in stay else pltpu.VMEM) for i in range(len(args))],
        scratch_shapes=list(scratch),
        name=body.__name__,
    )
    return run(*(a if i in stay else pltpu.with_memory_space_constraint(a, pltpu.VMEM) for i, a in enumerate(args)))


def dot(a, b, dims=((1,), (0,))):
    return lax.dot_general(a, b, (dims, ((), ())), preferred_element_type=F32)


def iota(shape, axis):
    return lax.broadcasted_iota(jnp.int32, shape, axis)


def ones(mask):
    return jnp.where(mask, F32(1.0), F32(0.0)).astype(BF16)


def swap_halves(x, y):
    low = iota(x.shape, 1) < HALF
    first = jnp.where(low, x, pltpu.roll(y, HALF, 1))
    second = jnp.where(low, pltpu.roll(x, HALF, 1), y)
    return first, second


def spread(load, store, pick_ref, weight_ref, moved_ref):
    count = moved_ref.shape[0] // BLOCKS
    pick = pick_ref[...]
    for g in range(0, count, GROUP):
        group = [jnp.concatenate(swap_halves(load(2 * p), load(2 * p + 1)), axis=0) for p in range(g, g + GROUP)]
        moved = dot(pick, jnp.concatenate(group, axis=1).astype(BF16)).astype(BF16)
        for i in range(GROUP):
            for k in range(pick.shape[0] // BLOCKS):
                moved_ref[pl.ds((g + i) * BLOCKS, BLOCKS), pl.ds(k * LANES, LANES)] = moved[
                    k * BLOCKS : (k + 1) * BLOCKS, i * LANES : (i + 1) * LANES
                ]
        out = dot(moved_ref[pl.ds(g * BLOCKS, GROUP * BLOCKS), :], weight_ref[...])
        for p in range(GROUP):
            at = p * BLOCKS
            x, y = swap_halves(out[at : at + PAIRS], out[at + PAIRS : at + BLOCKS])
            store(2 * (g + p), x)
            store(2 * (g + p) + 1, y)


def gather(load, loaded, source, send_ref, weight_ref, halves, moved):
    count, rows = send_ref.shape[:2]
    low = iota((rows, LANES), 1) < HALF
    for j in range(count):
        x = load(j)
        y = pltpu.roll(x, HALF, 1)
        halves[2 * j, :rows] = jnp.where(low, x, 0.0).astype(BF16)
        halves[2 * j + 1, :rows] = jnp.where(low, y, 0.0).astype(BF16)
        halves[BLOCKS + 2 * j, :rows] = jnp.where(low, 0.0, y).astype(BF16)
        halves[BLOCKS + 2 * j + 1, :rows] = jnp.where(low, 0.0, x).astype(BF16)
    loaded()
    deep = moved.shape[0] // count
    for j in range(count):
        for h in range(2):
            for k in range(0, weight_ref.shape[0] // LANES, 2):
                both = halves[source(k, 2 * j + h), :rows] + halves[BLOCKS + source(k + 1, 2 * j + h), :rows]
                at = (h * (weight_ref.shape[0] // LANES) + k) // 2
                moved[pl.ds(j * deep, rows), pl.ds(at * LANES, LANES)] = both
    some = count // 2
    for g in range(0, count, some):
        out = dot(moved[pl.ds(g * deep, some * deep), :], weight_ref[...])
        for i in range(some):
            send_ref[g + i] = out[i * deep : i * deep + rows].astype(BF16)


def open_chunks(recv_ref, flat):
    rows = recv_ref.shape[1]
    for j in range(recv_ref.shape[0]):
        flat[pl.ds(j * rows, rows), :] = recv_ref[j].astype(F32)


def close_chunks(flat, send_ref):
    rows = send_ref.shape[1]
    for j in range(send_ref.shape[0]):
        send_ref[j] = flat[pl.ds(j * rows, rows), :].astype(BF16)


def by_row(flat, rows):
    at = lambda r: pl.ds(r, PAIRS, stride=rows)

    def load(r):
        return flat[at(r), :]

    def store(r, x):
        flat[at(r), :] = x

    return load, store


def forward_first(
    control_hbm,
    offset_hbm,
    tiles_hbm,
    send_ref,
    kept_hbm,
    flat,
    moved,
    weight,
    kept,
    control,
    halves,
    offset_ref,
    tiles_ref,
    sems,
):
    members, variables, levels, columns = control.shape
    rows = send_ref.shape[1]
    fetch = [pltpu.make_async_copy(control_hbm.at[m], control.at[m], sems.at[m]) for m in range(members)]
    small = [
        pltpu.make_async_copy(offset_hbm, offset_ref, sems.at[members + 1]),
        pltpu.make_async_copy(tiles_hbm, tiles_ref, sems.at[members + 2]),
    ]
    for copy in fetch + small:
        copy.start()
    small[1].wait()
    wide = (HALF, LANES)
    places = ones(iota(wide, 1) == iota(wide, 0)), ones(iota(wide, 1) == iota(wide, 0) + HALF)
    slots = tiles_ref.shape[0]
    for h, place in enumerate(places):
        for k in range(slots):
            weight[pl.ds((h * slots + k) * HALF, HALF), :] = dot(tiles_ref[k], place).astype(BF16)
    for m in range(members):
        fetch[m].wait()
        for v in range(variables):
            x = control[m, v].astype(F32)
            at = (m * variables + v) * levels
            for j in range(columns // LANES):
                flat[pl.ds(j * rows + at, levels), :] = x[:, j * LANES : (j + 1) * LANES]

    def load(j):
        x = flat[pl.ds(j * rows, rows), :]
        kept[j] = x.astype(BF16)
        return x

    keep = pltpu.make_async_copy(kept, kept_hbm, sems.at[members])
    small[0].wait()
    source = lambda k, b: (b + offset_ref[k, b]) & (BLOCKS - 1)
    gather(load, keep.start, source, send_ref, weight, halves, moved)
    keep.wait()


def by_variable(recv_ref, variables):
    deep = recv_ref.shape[1] // variables
    field = recv_ref[...].astype(F32)
    return [field[:, v * deep : (v + 1) * deep, :].reshape(-1, LANES) for v in range(variables)]


def descend_static(grad_ref, root_ref, static_ref, next_ref):
    for v, grad in enumerate(by_variable(grad_ref, static_ref.shape[0])):
        current = static_ref[v].astype(F32)
        slope = current + STATIC_WEIGHT * dot(root_ref[v], grad.astype(BF16))
        next_ref[v] = (current - TAU * slope).astype(BF16)


def backward_forward(
    recv_ref,
    kept_ref,
    pick_t_ref,
    weight_t_ref,
    grad_ref,
    root_ref,
    static_ref,
    source_hbm,
    weight_ref,
    send_ref,
    next_hbm,
    moving_hbm,
    flat,
    moved,
    next_ref,
    moving_ref,
    halves,
    moved_ahead,
    source_ref,
    sems,
):
    fetch = pltpu.make_async_copy(source_hbm, source_ref, sems.at[2])
    fetch.start()
    descend_static(grad_ref, root_ref, static_ref, moving_ref)
    keep_static = pltpu.make_async_copy(moving_ref, moving_hbm, sems.at[0])
    keep_static.start()
    rows = recv_ref.shape[1]
    load, store = by_row(flat, rows)
    open_chunks(recv_ref, flat)
    spread(load, store, pick_t_ref, weight_t_ref, moved)

    def update(j):
        current = kept_ref[j].astype(F32)
        x = (current - TAU * (current + flat[pl.ds(j * rows, rows), :])).astype(BF16)
        next_ref[j] = x
        return x.astype(F32)

    keep = pltpu.make_async_copy(next_ref, next_hbm, sems.at[1])
    fetch.wait()
    gather(update, keep.start, lambda k, b: source_ref[k, b], send_ref, weight_ref, halves, moved_ahead)
    keep_static.wait()
    keep.wait()


def backward_last(
    recv_ref,
    kept_ref,
    pick_t_ref,
    weight_t_ref,
    grad_ref,
    root_ref,
    static_ref,
    control_hbm,
    moving_hbm,
    flat,
    moved,
    final,
    control,
    moving_ref,
    sems,
):
    members, variables, levels, columns = control.shape
    descend_static(grad_ref, root_ref, static_ref, moving_ref)
    keep_static = pltpu.make_async_copy(moving_ref, moving_hbm, sems.at[members])
    keep_static.start()
    rows = recv_ref.shape[1]
    load, store = by_row(flat, rows)
    open_chunks(recv_ref, flat)
    spread(load, store, pick_t_ref, weight_t_ref, moved)
    for j in range(columns // LANES):
        current = kept_ref[j].astype(F32)
        final[pl.ds(j * rows, rows), :] = current - TAU * (current + flat[pl.ds(j * rows, rows), :])
    copies = [pltpu.make_async_copy(control.at[m], control_hbm.at[m], sems.at[m]) for m in range(members)]
    for m in range(members):
        for v in range(variables):
            at = (m * variables + v) * levels
            for j in range(columns // LANES):
                x = final[pl.ds(j * rows + at, levels), :]
                control[m, v, :, pl.ds(j * LANES, LANES)] = x.astype(BF16)
        copies[m].start()
    keep_static.wait()
    for copy in copies:
        copy.wait()


def ensemble(recv_ref, perturb_ref, vert_ref, send_ref, flat):
    members, variables = perturb_ref.shape[:2]
    rows = recv_ref.shape[1]
    levels = rows // (members * variables)
    load, _ = by_row(flat, rows)
    open_chunks(recv_ref, flat)
    totals = []
    for v in range(variables):
        total = None
        for m in range(members):
            start = (m * variables + v) * levels
            x = jnp.concatenate([load(start + i) for i in range(levels)], axis=0).astype(BF16)
            term = dot(vert_ref[v], x, ((0,), (0,))) * perturb_ref[m, v].astype(F32)
            total = term if total is None else total + term
        totals.append(total)
    deep = send_ref.shape[1] // variables
    for d in range(send_ref.shape[0]):
        send_ref[d] = jnp.concatenate([t[d * deep : (d + 1) * deep] for t in totals], axis=0).astype(send_ref.dtype)


def observations(index_ref, value_ref, sigma_ref, mask_ref, slope_ref, shift_ref):
    cells = slope_ref.shape[0]
    weights = jnp.where(mask_ref[...] == 1, F32(1.0), F32(HUBER_LOW))
    precision = weights / (sigma_ref[...] * sigma_ref[...])
    pulled = precision * value_ref[...]
    index = index_ref[...]
    lefts, rights = [], []
    for o in range(index.shape[0]):
        at = index[o : o + 1]
        row = iota((cells, LANES), 0) == at // LANES
        lane = iota((LANES, LANES), 0) == at % LANES
        lefts.append(
            jnp.concatenate(
                [jnp.where(row, precision[o : o + 1], 0.0), jnp.where(row, pulled[o : o + 1], 0.0)], axis=0
            )
        )
        rights.append(jnp.where(lane, F32(1.0), F32(0.0)))
    both = lax.dot_general(
        jnp.concatenate(lefts, axis=1),
        jnp.concatenate(rights, axis=1),
        (((1,), (1,)), ((), ())),
        precision=lax.Precision.HIGHEST,
        preferred_element_type=F32,
    )
    slope_ref[...] = both[:cells]
    shift_ref[...] = both[cells:]


def gradient(recv_ref, static_ref, root_ref, slope_ref, shift_ref, send_ref, *, gain):
    ens = jnp.sum(recv_ref[...].astype(F32), axis=0)
    static = jnp.concatenate([dot(root_ref[v], static_ref[v]) for v in range(static_ref.shape[0])], axis=0)
    increment = gain * ens + STATIC_WEIGHT * static
    grad = (slope_ref[...] * increment - shift_ref[...]).astype(send_ref.dtype)
    for d in range(send_ref.shape[0]):
        send_ref[d] = grad


def backward(recv_ref, perturb_ref, vert_ref, send_ref, flat, *, gain):
    members, variables = perturb_ref.shape[:2]
    rows = send_ref.shape[1]
    levels = rows // (members * variables)
    _, store = by_row(flat, rows)
    grads = by_variable(recv_ref, variables)
    for v in range(variables):
        for m in range(members):
            weighted = (gain * grads[v]) * perturb_ref[m, v].astype(F32)
            high = weighted.astype(BF16)
            low = (weighted - high.astype(F32)).astype(BF16)
            back = dot(vert_ref[v], high) + dot(vert_ref[v], low)
            start = (m * variables + v) * levels
            for i in range(levels):
                store(start + i, back[i * PAIRS : (i + 1) * PAIRS])
    close_chunks(flat, send_ref)


def tables(block_offset):
    count, slots = block_offset.shape
    blocks = jnp.arange(count, dtype=jnp.int32)
    source = (blocks[:, None] + block_offset) % count
    spot = (source % 2) * (count // 2) + source // 2
    by_slot = spot.reshape(count // 2, 2, slots).transpose(2, 1, 0)
    back = (by_slot.reshape(slots, 1, count) == blocks[None, :, None]).reshape(slots * count, count)
    return source.T, back.astype(BF16)


def weights(tiles):
    width = tiles.shape[1]
    left = jnp.pad(tiles, ((0, 0), (0, 0), (0, width)))
    right = jnp.pad(tiles, ((0, 0), (0, 0), (width, 0)))
    return left, right


def on_device(
    control,
    static_control_vector,
    perturb,
    tiles,
    block_offset,
    vert,
    static_vertical_root,
    obs_index,
    obs_value,
    obs_sigma,
    huber_mask,
):
    n_lev, n_mem = lax.axis_size("lev"), lax.axis_size("mem")
    members, variables, levels, columns = control.shape
    levels_all = vert.shape[1]
    deep = levels_all // n_mem
    rows = members * variables * levels
    slots = tiles.shape[0]
    gain = ENS_W / math.sqrt(members * n_mem)

    source, pick_t = tables(block_offset)
    weight = jnp.concatenate(weights(tiles), axis=0).reshape(-1, LANES)
    weight_t = jnp.stack(weights(jnp.swapaxes(tiles, 1, 2)), axis=1).reshape(-1, LANES)
    turned = vert.reshape(variables, levels_all, n_lev, levels).transpose(0, 3, 2, 1).reshape(vert.shape)
    own_root = lax.dynamic_slice_in_dim(static_vertical_root, lax.axis_index("mem") * deep, deep, 1)

    vmem, hbm = pltpu.VMEM, pltpu.HBM
    chunks = vmem((n_lev, rows, LANES), BF16)
    parts = vmem((n_mem, variables * deep, LANES), BF16)
    field = vmem((variables * deep, LANES), F32)
    kept = (PAIRS, rows, LANES)
    padded = -(-rows // 16) * 16
    halves = vmem((2 * BLOCKS, padded, LANES), BF16)
    moved_ahead = vmem((PAIRS * padded, slots * LANES), BF16)
    flat = vmem((n_lev * rows, LANES), F32)
    moved = vmem((n_lev * rows, slots * LANES), BF16)
    dma = pltpu.SemaphoreType.DMA
    flat_obs = lambda x: x.reshape(-1, LANES)
    across = lambda x, axis: lax.all_to_all(x, axis, 0, 0, tiled=True)

    send, held = call(
        forward_first,
        (chunks, hbm(kept, BF16)),
        (
            flat,
            moved_ahead,
            vmem((slots * LANES, LANES), BF16),
            vmem(kept, BF16),
            vmem(control.shape, BF16),
            halves,
            pltpu.SMEM((slots, BLOCKS), jnp.int32),
            vmem(tiles.shape, BF16),
            dma((members + 3,)),
        ),
        (control, block_offset.T, tiles),
        stay=(0, 1, 2),
    )
    slope, shift = call(
        observations,
        (field, field),
        (),
        (flat_obs(obs_index), flat_obs(obs_value), flat_obs(obs_sigma), flat_obs(huber_mask)),
    )
    root_t = jnp.swapaxes(static_vertical_root, 1, 2)
    recv, slope, shift, own_root, root_t, turned, source, pick_t, weight, weight_t = lax.optimization_barrier(
        (across(send, "lev"), slope, shift, own_root, root_t, turned, source, pick_t, weight, weight_t)
    )
    static = static_control_vector
    for turn in range(ITERS):
        partial = call(ensemble, parts, (flat,), (recv, perturb, turned))
        grad = call(
            gradient, parts, (), (across(partial, "mem"), static, own_root, slope, shift), gain=gain
        )
        grad = across(grad, "mem")
        send = call(backward, chunks, (flat,), (grad, perturb, turned), gain=gain)
        operands = (across(send, "lev"), held, pick_t, weight_t, grad, root_t, static)
        if turn + 1 < ITERS:
            send, held, static = call(
                backward_forward,
                (chunks, hbm(kept, BF16), hbm(static.shape, BF16)),
                (
                    flat,
                    moved,
                    vmem(kept, BF16),
                    vmem(static.shape, BF16),
                    halves,
                    moved_ahead,
                    pltpu.SMEM((slots, BLOCKS), jnp.int32),
                    dma((3,)),
                ),
                (*operands, source, weight),
                stay=(7,),
            )
            recv = across(send, "lev")
        else:
            control, static = call(
                backward_last,
                (hbm(control.shape, BF16), hbm(static.shape, BF16)),
                (
                    flat,
                    moved,
                    flat,
                    vmem(control.shape, BF16),
                    vmem(static.shape, BF16),
                    dma((members + 1,)),
                ),
                operands,
            )
    return (control, static)


def solution(mesh):
    placed = (
        P("mem", None, "lev", None),
        P(None, None, "lev"),
        P("mem", None, None, "lev"),
        P(),
        P(),
        P(),
        P(),
        P(("lev", "mem")),
        P(("lev", "mem")),
        P(("lev", "mem")),
        P(("lev", "mem")),
    )
    return jax.shard_map(
        on_device,
        mesh=mesh,
        in_specs=placed,
        out_specs=(P("mem", None, "lev", None), P(None, None, "lev")),
        check_vma=False,
    )
```

```python
import functools
import math

import jax
import jax.numpy as jnp
from jax import lax
from jax.experimental import pallas as pl
from jax.experimental.pallas import tpu as pltpu
from jax.sharding import PartitionSpec as P

ITERS = 2

ENS_W = 0.85
STATIC_WEIGHT = 0.5
TAU = 0.5
HUBER_LOW = 0.3

F32 = jnp.float32
BF16 = jnp.bfloat16
LANES = 128
HALF = 64
PAIRS = 32
BLOCKS = 64
STAGGER_NS = 6500
GROUP = 5


def call(body, out_shape, scratch, args, stay=(), **static):
    run = pl.pallas_call(
        functools.partial(body, **static),
        out_shape=out_shape,
        in_specs=[pl.BlockSpec(memory_space=pl.ANY if i in stay else pltpu.VMEM) for i in range(len(args))],
        scratch_shapes=list(scratch),
        name=body.__name__,
    )
    return run(*(a if i in stay else pltpu.with_memory_space_constraint(a, pltpu.VMEM) for i, a in enumerate(args)))


def dot(a, b, dims=((1,), (0,))):
    return lax.dot_general(a, b, (dims, ((), ())), preferred_element_type=F32)


def iota(shape, axis):
    return lax.broadcasted_iota(jnp.int32, shape, axis)


def ones(mask):
    return jnp.where(mask, F32(1.0), F32(0.0)).astype(BF16)


def swap_halves(x, y):
    low = iota(x.shape, 1) < HALF
    first = jnp.where(low, x, pltpu.roll(y, HALF, 1))
    second = jnp.where(low, pltpu.roll(x, HALF, 1), y)
    return first, second


def spread(load, store, pick_ref, weight_ref, moved_ref):
    count = moved_ref.shape[0] // BLOCKS
    pick = pick_ref[...]
    for g in range(0, count, GROUP):
        group = [jnp.concatenate(swap_halves(load(2 * p), load(2 * p + 1)), axis=0) for p in range(g, g + GROUP)]
        moved = dot(pick, jnp.concatenate(group, axis=1).astype(BF16)).astype(BF16)
        for i in range(GROUP):
            for k in range(pick.shape[0] // BLOCKS):
                moved_ref[pl.ds((g + i) * BLOCKS, BLOCKS), pl.ds(k * LANES, LANES)] = moved[
                    k * BLOCKS : (k + 1) * BLOCKS, i * LANES : (i + 1) * LANES
                ]
        out = dot(moved_ref[pl.ds(g * BLOCKS, GROUP * BLOCKS), :], weight_ref[...])
        for p in range(GROUP):
            at = p * BLOCKS
            x, y = swap_halves(out[at : at + PAIRS], out[at + PAIRS : at + BLOCKS])
            store(2 * (g + p), x)
            store(2 * (g + p) + 1, y)


def gather(load, loaded, source, send_ref, weight_ref, halves, moved):
    count, rows = send_ref.shape[:2]
    low = iota((rows, LANES), 1) < HALF
    for j in range(count):
        x = load(j)
        y = pltpu.roll(x, HALF, 1)
        halves[2 * j, :rows] = jnp.where(low, x, 0.0).astype(BF16)
        halves[2 * j + 1, :rows] = jnp.where(low, y, 0.0).astype(BF16)
        halves[BLOCKS + 2 * j, :rows] = jnp.where(low, 0.0, y).astype(BF16)
        halves[BLOCKS + 2 * j + 1, :rows] = jnp.where(low, 0.0, x).astype(BF16)
    loaded()
    deep = moved.shape[0] // count
    for j in range(count):
        for h in range(2):
            for k in range(0, weight_ref.shape[0] // LANES, 2):
                both = halves[source(k, 2 * j + h), :rows] + halves[BLOCKS + source(k + 1, 2 * j + h), :rows]
                at = (h * (weight_ref.shape[0] // LANES) + k) // 2
                moved[pl.ds(j * deep, rows), pl.ds(at * LANES, LANES)] = both
    some = count // 2
    for g in range(0, count, some):
        out = dot(moved[pl.ds(g * deep, some * deep), :], weight_ref[...])
        for i in range(some):
            send_ref[g + i] = out[i * deep : i * deep + rows].astype(BF16)


def open_chunks(recv_ref, flat):
    rows = recv_ref.shape[1]
    for j in range(recv_ref.shape[0]):
        flat[pl.ds(j * rows, rows), :] = recv_ref[j].astype(F32)


def close_chunks(flat, send_ref):
    rows = send_ref.shape[1]
    for j in range(send_ref.shape[0]):
        send_ref[j] = flat[pl.ds(j * rows, rows), :].astype(BF16)


def by_row(flat, rows):
    at = lambda r: pl.ds(r, PAIRS, stride=rows)

    def load(r):
        return flat[at(r), :]

    def store(r, x):
        flat[at(r), :] = x

    return load, store


def forward_first(
    control_hbm,
    offset_hbm,
    tiles_hbm,
    send_ref,
    kept_hbm,
    flat,
    moved,
    weight,
    kept,
    control,
    halves,
    offset_ref,
    tiles_ref,
    sems,
):
    members, variables, levels, columns = control.shape
    rows = send_ref.shape[1]
    fetch = [pltpu.make_async_copy(control_hbm.at[m], control.at[m], sems.at[m]) for m in range(members)]
    small = [
        pltpu.make_async_copy(offset_hbm, offset_ref, sems.at[members + 1]),
        pltpu.make_async_copy(tiles_hbm, tiles_ref, sems.at[members + 2]),
    ]
    for copy in fetch + small:
        copy.start()
    small[1].wait()
    wide = (HALF, LANES)
    places = ones(iota(wide, 1) == iota(wide, 0)), ones(iota(wide, 1) == iota(wide, 0) + HALF)
    slots = tiles_ref.shape[0]
    for h, place in enumerate(places):
        for k in range(slots):
            weight[pl.ds((h * slots + k) * HALF, HALF), :] = dot(tiles_ref[k], place).astype(BF16)
    for m in range(members):
        fetch[m].wait()
        for v in range(variables):
            x = control[m, v].astype(F32)
            at = (m * variables + v) * levels
            for j in range(columns // LANES):
                flat[pl.ds(j * rows + at, levels), :] = x[:, j * LANES : (j + 1) * LANES]

    def load(j):
        x = flat[pl.ds(j * rows, rows), :]
        kept[j] = x.astype(BF16)
        return x

    keep = pltpu.make_async_copy(kept, kept_hbm, sems.at[members])
    small[0].wait()
    source = lambda k, b: (b + offset_ref[k, b]) & (BLOCKS - 1)
    gather(load, keep.start, source, send_ref, weight, halves, moved)
    keep.wait()


def by_variable(recv_ref, variables):
    deep = recv_ref.shape[1] // variables
    field = recv_ref[...].astype(F32)
    return [field[:, v * deep : (v + 1) * deep, :].reshape(-1, LANES) for v in range(variables)]


def descend_static(grad_ref, root_ref, static_ref, next_ref):
    for v, grad in enumerate(by_variable(grad_ref, static_ref.shape[0])):
        current = static_ref[v].astype(F32)
        slope = current + STATIC_WEIGHT * dot(root_ref[v], grad.astype(BF16))
        next_ref[v] = (current - TAU * slope).astype(BF16)


def backward_forward(
    recv_ref,
    kept_ref,
    pick_t_ref,
    weight_t_ref,
    grad_ref,
    root_ref,
    static_ref,
    source_hbm,
    weight_ref,
    send_ref,
    next_hbm,
    moving_hbm,
    flat,
    moved,
    next_ref,
    moving_ref,
    halves,
    moved_ahead,
    source_ref,
    sems,
):
    fetch = pltpu.make_async_copy(source_hbm, source_ref, sems.at[2])
    fetch.start()
    descend_static(grad_ref, root_ref, static_ref, moving_ref)
    keep_static = pltpu.make_async_copy(moving_ref, moving_hbm, sems.at[0])
    keep_static.start()
    rows = recv_ref.shape[1]
    load, store = by_row(flat, rows)
    open_chunks(recv_ref, flat)
    spread(load, store, pick_t_ref, weight_t_ref, moved)

    def update(j):
        current = kept_ref[j].astype(F32)
        x = (current - TAU * (current + flat[pl.ds(j * rows, rows), :])).astype(BF16)
        next_ref[j] = x
        return x.astype(F32)

    keep = pltpu.make_async_copy(next_ref, next_hbm, sems.at[1])
    fetch.wait()
    gather(update, keep.start, lambda k, b: source_ref[k, b], send_ref, weight_ref, halves, moved_ahead)
    keep_static.wait()
    keep.wait()


def backward_last(
    recv_ref,
    kept_ref,
    pick_t_ref,
    weight_t_ref,
    grad_ref,
    root_ref,
    static_ref,
    control_hbm,
    moving_hbm,
    flat,
    moved,
    final,
    control,
    moving_ref,
    sems,
):
    members, variables, levels, columns = control.shape
    descend_static(grad_ref, root_ref, static_ref, moving_ref)
    keep_static = pltpu.make_async_copy(moving_ref, moving_hbm, sems.at[members])
    keep_static.start()
    rows = recv_ref.shape[1]
    load, store = by_row(flat, rows)
    open_chunks(recv_ref, flat)
    spread(load, store, pick_t_ref, weight_t_ref, moved)
    for j in range(columns // LANES):
        current = kept_ref[j].astype(F32)
        final[pl.ds(j * rows, rows), :] = current - TAU * (current + flat[pl.ds(j * rows, rows), :])
    copies = [pltpu.make_async_copy(control.at[m], control_hbm.at[m], sems.at[m]) for m in range(members)]
    for m in range(members):
        for v in range(variables):
            at = (m * variables + v) * levels
            for j in range(columns // LANES):
                x = final[pl.ds(j * rows + at, levels), :]
                control[m, v, :, pl.ds(j * LANES, LANES)] = x.astype(BF16)
        copies[m].start()
    keep_static.wait()
    for copy in copies:
        copy.wait()


def ensemble(recv_ref, perturb_ref, vert_ref, send_ref, flat):
    members, variables = perturb_ref.shape[:2]
    rows = recv_ref.shape[1]
    levels = rows // (members * variables)
    load, _ = by_row(flat, rows)
    open_chunks(recv_ref, flat)
    totals = []
    for v in range(variables):
        total = None
        for m in range(members):
            start = (m * variables + v) * levels
            x = jnp.concatenate([load(start + i) for i in range(levels)], axis=0).astype(BF16)
            term = dot(vert_ref[v], x, ((0,), (0,))) * perturb_ref[m, v].astype(F32)
            total = term if total is None else total + term
        totals.append(total)
    deep = send_ref.shape[1] // variables
    for d in range(send_ref.shape[0]):
        send_ref[d] = jnp.concatenate([t[d * deep : (d + 1) * deep] for t in totals], axis=0).astype(send_ref.dtype)


def observations(index_ref, value_ref, sigma_ref, mask_ref, slope_ref, shift_ref):
    cells = slope_ref.shape[0]
    weights = jnp.where(mask_ref[...] == 1, F32(1.0), F32(HUBER_LOW))
    precision = weights / (sigma_ref[...] * sigma_ref[...])
    pulled = precision * value_ref[...]
    index = index_ref[...]
    lefts, rights = [], []
    for o in range(index.shape[0]):
        at = index[o : o + 1]
        row = iota((cells, LANES), 0) == at // LANES
        lane = iota((LANES, LANES), 0) == at % LANES
        lefts.append(
            jnp.concatenate(
                [jnp.where(row, precision[o : o + 1], 0.0), jnp.where(row, pulled[o : o + 1], 0.0)], axis=0
            )
        )
        rights.append(jnp.where(lane, F32(1.0), F32(0.0)))
    both = lax.dot_general(
        jnp.concatenate(lefts, axis=1),
        jnp.concatenate(rights, axis=1),
        (((1,), (1,)), ((), ())),
        precision=lax.Precision.HIGHEST,
        preferred_element_type=F32,
    )
    slope_ref[...] = both[:cells]
    shift_ref[...] = both[cells:]


def gradient(recv_ref, static_ref, root_ref, slope_ref, shift_ref, send_ref, *, gain):
    ens = jnp.sum(recv_ref[...].astype(F32), axis=0)
    static = jnp.concatenate([dot(root_ref[v], static_ref[v]) for v in range(static_ref.shape[0])], axis=0)
    increment = gain * ens + STATIC_WEIGHT * static
    grad = (slope_ref[...] * increment - shift_ref[...]).astype(send_ref.dtype)
    for d in range(send_ref.shape[0]):
        send_ref[d] = grad


def backward(recv_ref, perturb_ref, vert_ref, send_ref, flat, *, gain, hold):
    members, variables = perturb_ref.shape[:2]
    rows = send_ref.shape[1]
    levels = rows // (members * variables)
    _, store = by_row(flat, rows)
    grads = by_variable(recv_ref, variables)
    for v in range(variables):
        for m in range(members):
            weighted = (gain * grads[v]) * perturb_ref[m, v].astype(F32)
            high = weighted.astype(BF16)
            low = (weighted - high.astype(F32)).astype(BF16)
            back = dot(vert_ref[v], high) + dot(vert_ref[v], low)
            start = (m * variables + v) * levels
            for i in range(levels):
                store(start + i, back[i * PAIRS : (i + 1) * PAIRS])
    close_chunks(flat, send_ref)
    if hold:

        @pl.when((lax.axis_index("mem") & 1) == 0)
        def _():
            pl.delay(hold)


def tables(block_offset):
    count, slots = block_offset.shape
    blocks = jnp.arange(count, dtype=jnp.int32)
    source = (blocks[:, None] + block_offset) % count
    spot = (source % 2) * (count // 2) + source // 2
    by_slot = spot.reshape(count // 2, 2, slots).transpose(2, 1, 0)
    back = (by_slot.reshape(slots, 1, count) == blocks[None, :, None]).reshape(slots * count, count)
    return source.T, back.astype(BF16)


def weights(tiles):
    width = tiles.shape[1]
    left = jnp.pad(tiles, ((0, 0), (0, 0), (0, width)))
    right = jnp.pad(tiles, ((0, 0), (0, 0), (width, 0)))
    return left, right


def on_device(
    control,
    static_control_vector,
    perturb,
    tiles,
    block_offset,
    vert,
    static_vertical_root,
    obs_index,
    obs_value,
    obs_sigma,
    huber_mask,
):
    n_lev, n_mem = lax.axis_size("lev"), lax.axis_size("mem")
    members, variables, levels, columns = control.shape
    levels_all = vert.shape[1]
    deep = levels_all // n_mem
    rows = members * variables * levels
    slots = tiles.shape[0]
    gain = ENS_W / math.sqrt(members * n_mem)

    source, pick_t = tables(block_offset)
    weight = jnp.concatenate(weights(tiles), axis=0).reshape(-1, LANES)
    weight_t = jnp.stack(weights(jnp.swapaxes(tiles, 1, 2)), axis=1).reshape(-1, LANES)
    turned = vert.reshape(variables, levels_all, n_lev, levels).transpose(0, 3, 2, 1).reshape(vert.shape)
    own_root = lax.dynamic_slice_in_dim(static_vertical_root, lax.axis_index("mem") * deep, deep, 1)

    vmem, hbm = pltpu.VMEM, pltpu.HBM
    chunks = vmem((n_lev, rows, LANES), BF16)
    parts = vmem((n_mem, variables * deep, LANES), BF16)
    field = vmem((variables * deep, LANES), F32)
    kept = (PAIRS, rows, LANES)
    padded = -(-rows // 16) * 16
    halves = vmem((2 * BLOCKS, padded, LANES), BF16)
    moved_ahead = vmem((PAIRS * padded, slots * LANES), BF16)
    flat = vmem((n_lev * rows, LANES), F32)
    moved = vmem((n_lev * rows, slots * LANES), BF16)
    dma = pltpu.SemaphoreType.DMA
    flat_obs = lambda x: x.reshape(-1, LANES)
    across = lambda x, axis: lax.all_to_all(x, axis, 0, 0, tiled=True)

    send, held = call(
        forward_first,
        (chunks, hbm(kept, BF16)),
        (
            flat,
            moved_ahead,
            vmem((slots * LANES, LANES), BF16),
            vmem(kept, BF16),
            vmem(control.shape, BF16),
            halves,
            pltpu.SMEM((slots, BLOCKS), jnp.int32),
            vmem(tiles.shape, BF16),
            dma((members + 3,)),
        ),
        (control, block_offset.T, tiles),
        stay=(0, 1, 2),
    )
    slope, shift = call(
        observations,
        (field, field),
        (),
        (flat_obs(obs_index), flat_obs(obs_value), flat_obs(obs_sigma), flat_obs(huber_mask)),
    )
    root_t = jnp.swapaxes(static_vertical_root, 1, 2)
    recv, slope, shift, own_root, root_t, turned, source, pick_t, weight, weight_t = lax.optimization_barrier(
        (across(send, "lev"), slope, shift, own_root, root_t, turned, source, pick_t, weight, weight_t)
    )
    static = static_control_vector
    for turn in range(ITERS):
        partial = call(ensemble, parts, (flat,), (recv, perturb, turned))
        grad = call(
            gradient, parts, (), (across(partial, "mem"), static, own_root, slope, shift), gain=gain
        )
        grad = across(grad, "mem")
        send = call(backward, chunks, (flat,), (grad, perturb, turned), gain=gain, hold=STAGGER_NS * (turn + 1 < ITERS))
        operands = (across(send, "lev"), held, pick_t, weight_t, grad, root_t, static)
        if turn + 1 < ITERS:
            send, held, static = call(
                backward_forward,
                (chunks, hbm(kept, BF16), hbm(static.shape, BF16)),
                (
                    flat,
                    moved,
                    vmem(kept, BF16),
                    vmem(static.shape, BF16),
                    halves,
                    moved_ahead,
                    pltpu.SMEM((slots, BLOCKS), jnp.int32),
                    dma((3,)),
                ),
                (*operands, source, weight),
                stay=(7,),
            )
            recv = across(send, "lev")
        else:
            control, static = call(
                backward_last,
                (hbm(control.shape, BF16), hbm(static.shape, BF16)),
                (
                    flat,
                    moved,
                    flat,
                    vmem(control.shape, BF16),
                    vmem(static.shape, BF16),
                    dma((members + 1,)),
                ),
                operands,
            )
    return (control, static)


def solution(mesh):
    placed = (
        P("mem", None, "lev", None),
        P(None, None, "lev"),
        P("mem", None, None, "lev"),
        P(),
        P(),
        P(),
        P(),
        P(("lev", "mem")),
        P(("lev", "mem")),
        P(("lev", "mem")),
        P(("lev", "mem")),
    )
    return jax.shard_map(
        on_device,
        mesh=mesh,
        in_specs=placed,
        out_specs=(P("mem", None, "lev", None), P(None, None, "lev")),
        check_vma=False,
    )
```

```python
import functools
import math

import jax
import jax.numpy as jnp
from jax import lax
from jax.experimental import pallas as pl
from jax.experimental.pallas import tpu as pltpu
from jax.sharding import PartitionSpec as P

ITERS = 2

ENS_W = 0.85
STATIC_WEIGHT = 0.5
TAU = 0.5
HUBER_LOW = 0.3

F32 = jnp.float32
BF16 = jnp.bfloat16
LANES = 128
HALF = 64
PAIRS = 32
BLOCKS = 64
STAGGER_NS = 6200
GROUP = 5


def call(body, out_shape, scratch, args, stay=(), **static):
    run = pl.pallas_call(
        functools.partial(body, **static),
        out_shape=out_shape,
        in_specs=[pl.BlockSpec(memory_space=pl.ANY if i in stay else pltpu.VMEM) for i in range(len(args))],
        scratch_shapes=list(scratch),
        name=body.__name__,
    )
    return run(*(a if i in stay else pltpu.with_memory_space_constraint(a, pltpu.VMEM) for i, a in enumerate(args)))


def dot(a, b, dims=((1,), (0,))):
    return lax.dot_general(a, b, (dims, ((), ())), preferred_element_type=F32)


def iota(shape, axis):
    return lax.broadcasted_iota(jnp.int32, shape, axis)


def ones(mask):
    return jnp.where(mask, F32(1.0), F32(0.0)).astype(BF16)


def swap_halves(x, y):
    low = iota(x.shape, 1) < HALF
    first = jnp.where(low, x, pltpu.roll(y, HALF, 1))
    second = jnp.where(low, pltpu.roll(x, HALF, 1), y)
    return first, second


def spread(load, store, pick_ref, weight_ref, moved_ref):
    count = moved_ref.shape[0] // BLOCKS
    pick = pick_ref[...]
    for g in range(0, count, GROUP):
        group = [jnp.concatenate(swap_halves(load(2 * p), load(2 * p + 1)), axis=0) for p in range(g, g + GROUP)]
        moved = dot(pick, jnp.concatenate(group, axis=1).astype(BF16)).astype(BF16)
        for i in range(GROUP):
            for k in range(pick.shape[0] // BLOCKS):
                moved_ref[pl.ds((g + i) * BLOCKS, BLOCKS), pl.ds(k * LANES, LANES)] = moved[
                    k * BLOCKS : (k + 1) * BLOCKS, i * LANES : (i + 1) * LANES
                ]
        out = dot(moved_ref[pl.ds(g * BLOCKS, GROUP * BLOCKS), :], weight_ref[...])
        for p in range(GROUP):
            at = p * BLOCKS
            x, y = swap_halves(out[at : at + PAIRS], out[at + PAIRS : at + BLOCKS])
            store(2 * (g + p), x)
            store(2 * (g + p) + 1, y)


def gather(load, loaded, source, send_ref, weight_ref, halves, moved):
    count, rows = send_ref.shape[:2]
    low = iota((rows, LANES), 1) < HALF
    for j in range(count):
        x = load(j)
        y = pltpu.roll(x, HALF, 1)
        halves[2 * j, :rows] = jnp.where(low, x, 0.0).astype(BF16)
        halves[2 * j + 1, :rows] = jnp.where(low, y, 0.0).astype(BF16)
        halves[BLOCKS + 2 * j, :rows] = jnp.where(low, 0.0, y).astype(BF16)
        halves[BLOCKS + 2 * j + 1, :rows] = jnp.where(low, 0.0, x).astype(BF16)
    loaded()
    deep = moved.shape[0] // count
    for j in range(count):
        for h in range(2):
            for k in range(0, weight_ref.shape[0] // LANES, 2):
                both = halves[source(k, 2 * j + h), :rows] + halves[BLOCKS + source(k + 1, 2 * j + h), :rows]
                at = (h * (weight_ref.shape[0] // LANES) + k) // 2
                moved[pl.ds(j * deep, rows), pl.ds(at * LANES, LANES)] = both
    some = count // 2
    for g in range(0, count, some):
        out = dot(moved[pl.ds(g * deep, some * deep), :], weight_ref[...])
        for i in range(some):
            send_ref[g + i] = out[i * deep : i * deep + rows].astype(BF16)


def open_chunks(recv_ref, flat):
    rows = recv_ref.shape[1]
    for j in range(recv_ref.shape[0]):
        flat[pl.ds(j * rows, rows), :] = recv_ref[j].astype(F32)


def close_chunks(flat, send_ref):
    rows = send_ref.shape[1]
    for j in range(send_ref.shape[0]):
        send_ref[j] = flat[pl.ds(j * rows, rows), :].astype(BF16)


def by_row(flat, rows):
    at = lambda r: pl.ds(r, PAIRS, stride=rows)

    def load(r):
        return flat[at(r), :]

    def store(r, x):
        flat[at(r), :] = x

    return load, store


def forward_first(
    control_hbm,
    offset_hbm,
    tiles_hbm,
    send_ref,
    kept_hbm,
    flat,
    moved,
    weight,
    kept,
    control,
    halves,
    offset_ref,
    tiles_ref,
    sems,
):
    members, variables, levels, columns = control.shape
    rows = send_ref.shape[1]
    fetch = [pltpu.make_async_copy(control_hbm.at[m], control.at[m], sems.at[m]) for m in range(members)]
    small = [
        pltpu.make_async_copy(offset_hbm, offset_ref, sems.at[members + 1]),
        pltpu.make_async_copy(tiles_hbm, tiles_ref, sems.at[members + 2]),
    ]
    for copy in fetch + small:
        copy.start()
    small[1].wait()
    wide = (HALF, LANES)
    places = ones(iota(wide, 1) == iota(wide, 0)), ones(iota(wide, 1) == iota(wide, 0) + HALF)
    slots = tiles_ref.shape[0]
    for h, place in enumerate(places):
        for k in range(slots):
            weight[pl.ds((h * slots + k) * HALF, HALF), :] = dot(tiles_ref[k], place).astype(BF16)
    for m in range(members):
        fetch[m].wait()
        for v in range(variables):
            x = control[m, v].astype(F32)
            at = (m * variables + v) * levels
            for j in range(columns // LANES):
                flat[pl.ds(j * rows + at, levels), :] = x[:, j * LANES : (j + 1) * LANES]

    def load(j):
        x = flat[pl.ds(j * rows, rows), :]
        kept[j] = x.astype(BF16)
        return x

    keep = pltpu.make_async_copy(kept, kept_hbm, sems.at[members])
    small[0].wait()
    source = lambda k, b: (b + offset_ref[k, b]) & (BLOCKS - 1)
    gather(load, keep.start, source, send_ref, weight, halves, moved)
    keep.wait()


def by_variable(recv_ref, variables):
    deep = recv_ref.shape[1] // variables
    field = recv_ref[...].astype(F32)
    return [field[:, v * deep : (v + 1) * deep, :].reshape(-1, LANES) for v in range(variables)]


def descend_static(grad_ref, root_ref, static_ref, next_ref):
    for v, grad in enumerate(by_variable(grad_ref, static_ref.shape[0])):
        current = static_ref[v].astype(F32)
        slope = current + STATIC_WEIGHT * dot(root_ref[v], grad.astype(BF16))
        next_ref[v] = (current - TAU * slope).astype(BF16)


def backward_forward(
    recv_ref,
    kept_ref,
    pick_t_ref,
    weight_t_ref,
    source_hbm,
    weight_ref,
    send_ref,
    next_hbm,
    flat,
    moved,
    next_ref,
    halves,
    moved_ahead,
    source_ref,
    sems,
):
    fetch = pltpu.make_async_copy(source_hbm, source_ref, sems.at[0])
    fetch.start()
    rows = recv_ref.shape[1]
    load, store = by_row(flat, rows)
    open_chunks(recv_ref, flat)
    spread(load, store, pick_t_ref, weight_t_ref, moved)

    def update(j):
        current = kept_ref[j].astype(F32)
        x = (current - TAU * (current + flat[pl.ds(j * rows, rows), :])).astype(BF16)
        next_ref[j] = x
        return x.astype(F32)

    keep = pltpu.make_async_copy(next_ref, next_hbm, sems.at[1])
    fetch.wait()
    gather(update, keep.start, lambda k, b: source_ref[k, b], send_ref, weight_ref, halves, moved_ahead)
    keep.wait()


def backward_last(
    recv_ref,
    kept_ref,
    pick_t_ref,
    weight_t_ref,
    grad_ref,
    root_ref,
    static_ref,
    control_hbm,
    moving_hbm,
    flat,
    moved,
    final,
    control,
    moving_ref,
    sems,
):
    members, variables, levels, columns = control.shape
    descend_static(grad_ref, root_ref, static_ref, moving_ref)
    keep_static = pltpu.make_async_copy(moving_ref, moving_hbm, sems.at[members])
    keep_static.start()
    rows = recv_ref.shape[1]
    load, store = by_row(flat, rows)
    open_chunks(recv_ref, flat)
    spread(load, store, pick_t_ref, weight_t_ref, moved)
    for j in range(columns // LANES):
        current = kept_ref[j].astype(F32)
        final[pl.ds(j * rows, rows), :] = current - TAU * (current + flat[pl.ds(j * rows, rows), :])
    copies = [pltpu.make_async_copy(control.at[m], control_hbm.at[m], sems.at[m]) for m in range(members)]
    for m in range(members):
        for v in range(variables):
            at = (m * variables + v) * levels
            for j in range(columns // LANES):
                x = final[pl.ds(j * rows + at, levels), :]
                control[m, v, :, pl.ds(j * LANES, LANES)] = x.astype(BF16)
        copies[m].start()
    keep_static.wait()
    for copy in copies:
        copy.wait()


def ensemble(recv_ref, perturb_ref, vert_ref, send_ref, flat):
    members, variables = perturb_ref.shape[:2]
    rows = recv_ref.shape[1]
    levels = rows // (members * variables)
    load, _ = by_row(flat, rows)
    open_chunks(recv_ref, flat)
    totals = []
    for v in range(variables):
        total = None
        for m in range(members):
            start = (m * variables + v) * levels
            x = jnp.concatenate([load(start + i) for i in range(levels)], axis=0).astype(BF16)
            term = dot(vert_ref[v], x, ((0,), (0,))) * perturb_ref[m, v].astype(F32)
            total = term if total is None else total + term
        totals.append(total)
    deep = send_ref.shape[1] // variables
    for d in range(send_ref.shape[0]):
        send_ref[d] = jnp.concatenate([t[d * deep : (d + 1) * deep] for t in totals], axis=0).astype(send_ref.dtype)


def observations(index_ref, value_ref, sigma_ref, mask_ref, slope_ref, shift_ref):
    cells = slope_ref.shape[0]
    weights = jnp.where(mask_ref[...] == 1, F32(1.0), F32(HUBER_LOW))
    precision = weights / (sigma_ref[...] * sigma_ref[...])
    pulled = precision * value_ref[...]
    index = index_ref[...]
    lefts, rights = [], []
    for o in range(index.shape[0]):
        at = index[o : o + 1]
        row = iota((cells, LANES), 0) == at // LANES
        lane = iota((LANES, LANES), 0) == at % LANES
        lefts.append(
            jnp.concatenate(
                [jnp.where(row, precision[o : o + 1], 0.0), jnp.where(row, pulled[o : o + 1], 0.0)], axis=0
            )
        )
        rights.append(jnp.where(lane, F32(1.0), F32(0.0)))
    both = lax.dot_general(
        jnp.concatenate(lefts, axis=1),
        jnp.concatenate(rights, axis=1),
        (((1,), (1,)), ((), ())),
        precision=lax.Precision.HIGHEST,
        preferred_element_type=F32,
    )
    slope_ref[...] = both[:cells]
    shift_ref[...] = both[cells:]


def gradient(recv_ref, static_ref, root_ref, slope_ref, shift_ref, send_ref, *, gain):
    ens = jnp.sum(recv_ref[...].astype(F32), axis=0)
    static = jnp.concatenate([dot(root_ref[v], static_ref[v]) for v in range(static_ref.shape[0])], axis=0)
    increment = gain * ens + STATIC_WEIGHT * static
    grad = (slope_ref[...] * increment - shift_ref[...]).astype(send_ref.dtype)
    for d in range(send_ref.shape[0]):
        send_ref[d] = grad


def backward_hold(recv_ref, perturb_ref, vert_ref, root_ref, static_ref, send_ref, next_ref, flat, *, gain, hold):
    backward(recv_ref, perturb_ref, vert_ref, send_ref, flat, gain=gain)
    descend_static(recv_ref, root_ref, static_ref, next_ref)

    @pl.when((lax.axis_index("mem") & 1) == 0)
    def _():
        pl.delay(hold)


def backward(recv_ref, perturb_ref, vert_ref, send_ref, flat, *, gain):
    members, variables = perturb_ref.shape[:2]
    rows = send_ref.shape[1]
    levels = rows // (members * variables)
    _, store = by_row(flat, rows)
    grads = by_variable(recv_ref, variables)
    for v in range(variables):
        for m in range(members):
            weighted = (gain * grads[v]) * perturb_ref[m, v].astype(F32)
            high = weighted.astype(BF16)
            low = (weighted - high.astype(F32)).astype(BF16)
            back = dot(vert_ref[v], high) + dot(vert_ref[v], low)
            start = (m * variables + v) * levels
            for i in range(levels):
                store(start + i, back[i * PAIRS : (i + 1) * PAIRS])
    close_chunks(flat, send_ref)


def tables(block_offset):
    count, slots = block_offset.shape
    blocks = jnp.arange(count, dtype=jnp.int32)
    source = (blocks[:, None] + block_offset) % count
    spot = (source % 2) * (count // 2) + source // 2
    by_slot = spot.reshape(count // 2, 2, slots).transpose(2, 1, 0)
    back = (by_slot.reshape(slots, 1, count) == blocks[None, :, None]).reshape(slots * count, count)
    return source.T, back.astype(BF16)


def weights(tiles):
    width = tiles.shape[1]
    left = jnp.pad(tiles, ((0, 0), (0, 0), (0, width)))
    right = jnp.pad(tiles, ((0, 0), (0, 0), (width, 0)))
    return left, right


def on_device(
    control,
    static_control_vector,
    perturb,
    tiles,
    block_offset,
    vert,
    static_vertical_root,
    obs_index,
    obs_value,
    obs_sigma,
    huber_mask,
):
    n_lev, n_mem = lax.axis_size("lev"), lax.axis_size("mem")
    members, variables, levels, columns = control.shape
    levels_all = vert.shape[1]
    deep = levels_all // n_mem
    rows = members * variables * levels
    slots = tiles.shape[0]
    gain = ENS_W / math.sqrt(members * n_mem)

    source, pick_t = tables(block_offset)
    weight = jnp.concatenate(weights(tiles), axis=0).reshape(-1, LANES)
    weight_t = jnp.stack(weights(jnp.swapaxes(tiles, 1, 2)), axis=1).reshape(-1, LANES)
    turned = vert.reshape(variables, levels_all, n_lev, levels).transpose(0, 3, 2, 1).reshape(vert.shape)
    own_root = lax.dynamic_slice_in_dim(static_vertical_root, lax.axis_index("mem") * deep, deep, 1)

    vmem, hbm = pltpu.VMEM, pltpu.HBM
    chunks = vmem((n_lev, rows, LANES), BF16)
    parts = vmem((n_mem, variables * deep, LANES), BF16)
    field = vmem((variables * deep, LANES), F32)
    kept = (PAIRS, rows, LANES)
    padded = -(-rows // 16) * 16
    halves = vmem((2 * BLOCKS, padded, LANES), BF16)
    moved_ahead = vmem((PAIRS * padded, slots * LANES), BF16)
    flat = vmem((n_lev * rows, LANES), F32)
    moved = vmem((n_lev * rows, slots * LANES), BF16)
    dma = pltpu.SemaphoreType.DMA
    flat_obs = lambda x: x.reshape(-1, LANES)
    across = lambda x, axis: lax.all_to_all(x, axis, 0, 0, tiled=True)

    send, held = call(
        forward_first,
        (chunks, hbm(kept, BF16)),
        (
            flat,
            moved_ahead,
            vmem((slots * LANES, LANES), BF16),
            vmem(kept, BF16),
            vmem(control.shape, BF16),
            halves,
            pltpu.SMEM((slots, BLOCKS), jnp.int32),
            vmem(tiles.shape, BF16),
            dma((members + 3,)),
        ),
        (control, block_offset.T, tiles),
        stay=(0, 1, 2),
    )
    slope, shift = call(
        observations,
        (field, field),
        (),
        (flat_obs(obs_index), flat_obs(obs_value), flat_obs(obs_sigma), flat_obs(huber_mask)),
    )
    root_t = jnp.swapaxes(static_vertical_root, 1, 2)
    recv, slope, shift, own_root, root_t, turned, source, pick_t, weight, weight_t = lax.optimization_barrier(
        (across(send, "lev"), slope, shift, own_root, root_t, turned, source, pick_t, weight, weight_t)
    )
    static = static_control_vector
    for turn in range(ITERS):
        partial = call(ensemble, parts, (flat,), (recv, perturb, turned))
        grad = call(
            gradient, parts, (), (across(partial, "mem"), static, own_root, slope, shift), gain=gain
        )
        grad = across(grad, "mem")
        if turn + 1 < ITERS:
            send, static = call(
                backward_hold,
                (chunks, vmem(static.shape, BF16)),
                (flat,),
                (grad, perturb, turned, root_t, static),
                gain=gain,
                hold=STAGGER_NS,
            )
            send, held = call(
                backward_forward,
                (chunks, hbm(kept, BF16)),
                (
                    flat,
                    moved,
                    vmem(kept, BF16),
                    halves,
                    moved_ahead,
                    pltpu.SMEM((slots, BLOCKS), jnp.int32),
                    dma((2,)),
                ),
                (across(send, "lev"), held, pick_t, weight_t, source, weight),
                stay=(4,),
            )
            recv = across(send, "lev")
        else:
            send = call(backward, chunks, (flat,), (grad, perturb, turned), gain=gain)
            operands = (across(send, "lev"), held, pick_t, weight_t, grad, root_t, static)
            control, static = call(
                backward_last,
                (hbm(control.shape, BF16), hbm(static.shape, BF16)),
                (
                    flat,
                    moved,
                    flat,
                    vmem(control.shape, BF16),
                    vmem(static.shape, BF16),
                    dma((members + 1,)),
                ),
                operands,
            )
    return (control, static)


def solution(mesh):
    placed = (
        P("mem", None, "lev", None),
        P(None, None, "lev"),
        P("mem", None, None, "lev"),
        P(),
        P(),
        P(),
        P(),
        P(("lev", "mem")),
        P(("lev", "mem")),
        P(("lev", "mem")),
        P(("lev", "mem")),
    )
    return jax.shard_map(
        on_device,
        mesh=mesh,
        in_specs=placed,
        out_specs=(P("mem", None, "lev", None), P(None, None, "lev")),
        check_vma=False,
    )
```
